32 devices in a mesh: dp: 16 (over z, y, core), tensor: 2 (over x).
Axes of the slice: x: 2, y: 2, z: 4, core: 2. Of those that a mesh axis runs over, the one named last changes fastest.
Arguments:
- tokens: bfloat16 [16384, 1024], P(('dp', 'tensor')), may hold values from -6 to 6
- norm1_gain: float32 [1024], replicated, may hold values from 0.5 to 1.5
- w_qkv: bfloat16 [1024, 1536], P(None, 'tensor'), may hold values from -0.1875 to 0.1875
- w_out: bfloat16 [1024, 1024], P('tensor'), may hold values from -2 to 2
- norm2_gain: float32 [1024], replicated, may hold values from 0.5 to 1.5
- w_gate_up: bfloat16 [2, 1024, 2752], P(None, None, 'tensor'), may hold values from -0.1875 to 0.1875
- w_down: bfloat16 [2752, 1024], P('tensor'), may hold values from -0.109375 to 0.109375
- cotangent: bfloat16 [16384, 1024], P(('dp', 'tensor')), may hold values from -6 to 6
- old_mean: float32 [1], replicated, may hold values from 1.5 to 3
- momentum: float32 [1], replicated, may hold values from 0.5 to 0.9
Outputs:
- output: bfloat16 [16384, 1024], P(('dp', 'tensor'))
- input_grad: float32 [16384, 1024], P(('dp', 'tensor'))
- grad_norm1_gain: float32 [1024], replicated
- grad_w_qkv: float32 [1024, 1536], P(None, 'tensor')
- grad_w_out: float32 [1024, 1024], P('tensor')
- grad_norm2_gain: float32 [1024], replicated
- grad_w_gate_up: float32 [2, 1024, 2752], P(None, None, 'tensor')
- grad_w_down: float32 [2752, 1024], P('tensor')
- new_mean: float32 [1], replicated
The draws below stay inside these ranges and needn't reach their ends.
All inputs are finite; a program needn't handle non-finite values.
Results may differ from the reference program's by a relative error of at most 0.0095.
The reference program's roundings to bfloat16 on the way count: a program that leaves them out, or rounds other values in their place, can miss the bound.
Values may be sent and summed in bfloat16 or wider, within the bound.
No kernel may reach another device: no remote copies, remote signals or barrier semaphores. Data moves between devices by JAX's collectives and lax.ppermute only.
A program may use at most 192 MiB of HBM per device.

```python
import math
import jax
import jax.numpy as jnp
from jax import lax

D = 1024
H = 16
F = 16
V = 64
FF = 2752
SEQ = 1024
BLK = 512
TOKENS = 16384
N_DP = 16


def steps_of(stream_key, dims, pieces, low, largest):
    def one(dim, parts):
        draws = jax.random.uniform(jax.random.fold_in(jax.random.fold_in(stream_key, 6), dim), (parts,), jnp.float32, low / len(pieces), largest / len(pieces))
        return jnp.repeat(jnp.exp(draws), dims[dim] // parts).reshape((-1,) + (1,) * (len(dims) - dim - 1))

    level = one(*pieces[0])
    for cut in pieces[1:]:
        level = level * one(*cut)
    return level


def normal_values(rng, shape, deviation, reach, pieces=(), kind=jnp.bfloat16):
    values = jax.random.normal(rng, shape, jnp.float32) * deviation
    if len(pieces) > 0:
        values = steps_of(rng, shape, pieces, -0.22, 0.18) * values
    return jnp.clip(values, min=-reach, max=reach).astype(kind)


def setup_inputs(seed: int = 0) -> dict:
    key_of = jax.random.split(jax.random.key(seed), 11)
    tokens = normal_values(key_of[0], (TOKENS, D), 1.0, 6.0, ((0, 32),))
    norm1_gain = jnp.clip(1.0 + 0.1 * jax.random.normal(key_of[1], (D,), jnp.float32), 0.5, 1.5)
    w_qkv = normal_values(key_of[2], (D, H * (2 * F + V)), D ** -0.5, 0.1875, ((1, 2),))
    w_out = normal_values(key_of[3], (H * V, D), 8 ** -0.5, 2.0, ((0, 2),))
    norm2_gain = jnp.clip(1.0 + 0.1 * jax.random.normal(key_of[4], (D,), jnp.float32), 0.5, 1.5)
    w_gate_up = normal_values(key_of[5], (2, D, FF), D ** -0.5, 0.1875, ((2, 2),))
    w_down = normal_values(key_of[6], (FF, D), FF ** -0.5, 0.109375, ((0, 2),))
    cotangent = normal_values(key_of[7], (TOKENS, D), 1.0, 6.0, ((0, 32),))
    old_mean = jnp.clip(jax.random.uniform(key_of[8], (1,), jnp.float32, 1.5, 3.0), 1.5, 3.0)
    momentum = jnp.clip(jax.random.uniform(key_of[9], (1,), jnp.float32, 0.5, 0.9), 0.5, 0.9)
    return dict(tokens=tokens, norm1_gain=norm1_gain, w_qkv=w_qkv, w_out=w_out, norm2_gain=norm2_gain, w_gate_up=w_gate_up, w_down=w_down, cotangent=cotangent, old_mean=old_mean, momentum=momentum)


@jax.custom_vjp
def low(v):
    return lax.optimization_barrier(v.astype(jnp.bfloat16)).astype(jnp.float32)

@jax.custom_vjp
def low_back(v):
    return v

def low_keep(v):
    return (low(v), None)

def low_pass(kept, grad):
    return (grad,)

def back_keep(v):
    return (v, None)

def back_low(kept, grad):
    return (low(grad),)
low.defvjp(low_keep, low_pass)
low_back.defvjp(back_keep, back_low)
PRECISE = lax.Precision.HIGHEST
EPSILON = 1e-05

def features(vector):
    width = vector.shape[-1]
    ones = jnp.ones(vector.shape[:-1] + (1,), jnp.float32)
    outer = (vector[..., :, None] * vector[..., None, :]).reshape(vector.shape[:-1] + (width * width,))
    return jnp.concatenate([ones, vector * width ** (-0.25), outer * (0.5 ** 0.5 / width ** 0.5)], axis=-1)

def attend(query, keys, values):
    length, heads, width = query.shape
    value_width = values.shape[-1]
    blocks = length // BLK
    query_blocks = query.reshape(blocks, BLK, heads, width)
    key_blocks = keys.reshape(blocks, BLK, heads, width)
    value_blocks = values.reshape(blocks, BLK, heads, value_width)
    causal = (jnp.arange(BLK)[:, None] >= jnp.arange(BLK)[None, :]).astype(jnp.float32)
    nfeat = 1 + width + width * width

    def step(carry, block):
        state, total = carry
        query_part, key_part, value_part = block
        scores = jnp.einsum('ihf,jhf->hij', query_part, key_part, precision=PRECISE) / math.sqrt(width)
        weight = (1.0 + scores + 0.5 * scores * scores) * causal
        query_feat = features(query_part)
        key_feat = features(key_part)
        numer = jnp.einsum('hij,jhv->ihv', weight, value_part, precision=PRECISE)
        numer = numer + jnp.einsum('ihp,hpv->ihv', query_feat, state, precision=PRECISE)
        denom = lax.optimization_barrier(jnp.sum(weight, axis=2)).T + jnp.einsum('ihp,hp->ih', query_feat, total, precision=PRECISE)
        state = state + jnp.einsum('jhp,jhv->hpv', key_feat, value_part, precision=PRECISE)
        total = total + lax.optimization_barrier(jnp.sum(key_feat, axis=0))
        return ((state, total), (numer / denom[..., None], denom))
    start_state = (jnp.zeros((heads, nfeat, value_width), jnp.float32), jnp.zeros((heads, nfeat), jnp.float32))
    final_state, (result, denoms) = lax.scan(jax.checkpoint(step), start_state, (query_blocks, key_blocks, value_blocks))
    return (result.reshape(length, heads, value_width), denoms.reshape(length, heads))

def rms_norm(rows, gain):
    return rows * lax.rsqrt(lax.optimization_barrier(jnp.mean(rows * rows, axis=-1, keepdims=True)) + EPSILON) * gain

def forward(params, rows):
    gain1, w_qkv, w_out, gain2, w_gate_up, w_down = params
    length = rows.shape[0]
    width = 2 * F + V
    heads = w_qkv.shape[1] // width
    normed = low(rms_norm(rows, gain1))
    packed = low(low_back(jnp.dot(normed, w_qkv, precision=PRECISE))).reshape(length, heads, width)
    attended, denoms = attend(packed[..., :F], packed[..., F:2 * F], packed[..., 2 * F:])
    mixer_in = low(low_back(attended.reshape(length, heads * V)))
    resid = rows + low_back(jnp.dot(mixer_in, w_out, precision=PRECISE))
    normed2 = low(rms_norm(resid, gain2))
    gate = low_back(jnp.dot(normed2, w_gate_up[0], precision=PRECISE))
    upward = low_back(jnp.dot(normed2, w_gate_up[1], precision=PRECISE))
    hidden = low(low_back(jax.nn.silu(gate) * upward))
    return (resid + jnp.dot(hidden, w_down, precision=PRECISE), jnp.sum(denoms))

def reference(tokens, norm1_gain, w_qkv, w_out, norm2_gain, w_gate_up, w_down, cotangent, old_mean, momentum):
    params = (norm1_gain.astype(jnp.float32), w_qkv.astype(jnp.float32), w_out.astype(jnp.float32), norm2_gain.astype(jnp.float32), w_gate_up.astype(jnp.float32), w_down.astype(jnp.float32))
    inputs_all = tokens.astype(jnp.float32).reshape(N_DP, SEQ, D)
    upstream_all = cotangent.astype(jnp.float32).reshape(N_DP, SEQ, D)
    zero_grads = jax.tree.map(jnp.zeros_like, params)

    def one_sequence(carry, item):
        gradients, denom_total = carry
        seq_rows, seq_upstream = item
        result, backward, denom_sum = jax.vjp(forward, params, seq_rows, has_aux=True)
        param_grads, rows_grad = backward(seq_upstream)
        gradients = jax.tree.map(lambda left, right: left + right, gradients, param_grads)
        return ((gradients, denom_total + denom_sum), (result, rows_grad))
    (gradients, denom_total), (results, rows_grads) = lax.scan(one_sequence, (zero_grads, jnp.zeros((), jnp.float32)), (inputs_all, upstream_all))
    mean_value = denom_total / TOKENS / (H * SEQ)
    new_mean = momentum * old_mean + (1.0 - momentum) * mean_value
    return (results.reshape(TOKENS, D).astype(jnp.bfloat16), rows_grads.reshape(TOKENS, D), gradients[0], gradients[1], gradients[2], gradients[3], gradients[4], gradients[5], new_mean)
```

```python
import functools

import jax
import jax.numpy as jnp
from jax import lax
from jax.experimental import pallas as pl
from jax.experimental.pallas import tpu as pltpu
from jax.sharding import PartitionSpec as P

F = 16
V = 64
EPSILON = 1e-05
F32 = jnp.float32
BF = jnp.bfloat16
NT = (((1,), (1,)), ((), ()))
NN = (((1,), (0,)), ((), ()))
TN = (((0,), (0,)), ((), ()))
LANES = 128
COST = pl.CostEstimate(flops=5 * 10**10, bytes_accessed=10**8, transcendentals=0)
SMALL = COST
FAST = (
    "gudtGUDwGAUDWGAKqUDWG"
    "QUDGNOQUDGsoQsGUDQsUDQsQsQ"
)


def after(x, *others):
    return lax.optimization_barrier((x, *others))[0]


def dg(a, b, dims):
    return lax.dot_general(a, b, dims, preferred_element_type=F32)


def attend_fwd_body(blk, per, base, me_ref, q_ref, k_ref, v_ref, own_ref, sent_ref, attf_ref, den_ref, sum_ref, vals, att_s):
    length = q_ref.shape[0]
    n = length // blk
    pair = pl.program_id(0)
    flip = me_ref[0] * per

    def at(b):
        return pl.ds(pl.multiple_of((b ^ flip) * blk, blk), blk)

    vals[:, :LANES] = v_ref[...]
    eights = jnp.zeros((8, LANES), F32)

    @pl.when(pair == 0)
    def _():
        vals[:, LANES:] = jnp.ones((length, LANES), BF)

    lane = lax.broadcasted_iota(jnp.int32, (blk, LANES), 1)
    row = lax.broadcasted_iota(jnp.int32, (blk, blk), 0)
    col = lax.broadcasted_iota(jnp.int32, (blk, blk), 1)
    for i in range(n):
        query = q_ref[at(i), :]
        sums = []
        for side in range(2):
            mine = jnp.where(lane // F == 2 * (base + pair) + side, query * 0.25, 0).astype(BF)
            total = None
            for j in range(i + 1):
                t = 1.0 + dg(mine, k_ref[at(j), :], NT)
                a = t * t + 1.0
                if j == i:
                    a = jnp.where(row >= col, a, 0.0)
                part = dg(a.astype(BF), vals[at(j), :], NN)
                total = part if total is None else total + part
            sums.append(total)
        numer = jnp.where(lane < V, sums[0][:, :LANES], sums[1][:, :LANES])
        denom = jnp.where(lane < V, sums[0][:, LANES:], sums[1][:, LANES:])
        att = numer / denom
        att_s[at(i), :] = att.astype(BF)
        attf_ref[at(i), :] = att
        den_ref[at(i), :] = denom
        eights = eights + jnp.sum(denom.reshape(-1, 8, LANES), axis=0)
    sum_ref[...] = eights
    rows = own_ref.shape[0]
    own_ref[...] = att_s[:rows, :]
    sent_ref[...] = att_s[rows:, :]


def attend_fwd(packed, me, heads, qw, blk, per, base, pairs):
    length = packed.shape[0]
    rows = blk * per
    skip = 2 * qw // LANES + base
    spec = lambda index, n=length: pl.BlockSpec((n, LANES), index)
    column = lambda p, m: (0, p)
    width = LANES * pairs
    return pl.pallas_call(
        functools.partial(attend_fwd_body, blk, per, base),
        grid_spec=pltpu.PrefetchScalarGridSpec(
            num_scalar_prefetch=1,
            grid=(pairs,),
            in_specs=[
                spec(lambda p, m: (0, 0)),
                spec(lambda p, m: (0, 1)),
                spec(lambda p, m: (0, skip + p)),
            ],
            out_specs=[
                spec(column, rows),
                spec(column, length - rows),
                spec(column),
                spec(column),
                spec(column, 8),
            ],
            scratch_shapes=[pltpu.VMEM((length, 2 * LANES), BF), pltpu.VMEM((length, LANES), BF)],
        ),
        out_shape=[
            jax.ShapeDtypeStruct((rows, width), BF),
            jax.ShapeDtypeStruct((length - rows, width), BF),
            jax.ShapeDtypeStruct((length, width), F32),
            jax.ShapeDtypeStruct((length, width), F32),
            jax.ShapeDtypeStruct((8, width), F32),
        ],
        cost_estimate=COST,
        name="attend_fwd",
    )(me, packed, packed, packed)


def attend_bwd_body(blk, per, qw, base, me_ref, q_ref, k_ref, v_ref, g_own, g_sent, attf_ref, den_ref, *refs):
    out_ref, dq, q_t, g_t, dk_t, g_ref = refs[-6:]
    length = q_ref.shape[0]
    n = length // blk
    step = pl.program_id(0)
    pair = base + step
    flip = me_ref[0] * per

    def at(b):
        return pl.ds(pl.multiple_of((b ^ flip) * blk, blk), blk)

    lane = lax.broadcasted_iota(jnp.int32, (blk, LANES), 1)
    row = lax.broadcasted_iota(jnp.int32, (blk, blk), 0)
    col = lax.broadcasted_iota(jnp.int32, (blk, blk), 1)
    halves = (lane < V, lane >= V)

    @pl.when(step == 0)
    def _():
        q_t[...] = q_ref[...].T
        if base == 0:
            dq[...] = jnp.zeros_like(dq)
            dk_t[...] = jnp.zeros_like(dk_t)
        else:
            before = refs[0]
            dq[...] = before[:, :qw].astype(F32)
            dk_t[...] = before[:, qw : 2 * qw].astype(F32).T
            done = 2 * qw + LANES * base
            out_ref[:, 2 * qw : done] = before[:, 2 * qw : done]

    rows = g_own.shape[0]
    g_ref[:rows, :] = g_own[...]
    g_ref[rows:, :] = g_sent[...]
    scale = []
    for i in range(n):
        g = g_ref[at(i), :].astype(F32)
        inv = 1.0 / den_ref[at(i), :]
        ga = g * attf_ref[at(i), :]
        g_t[:, i * blk : (i + 1) * blk] = (g * inv).astype(BF).T
        for side in range(2):
            c = jnp.sum(jnp.where(halves[side], ga, 0.0), axis=1, keepdims=True)
            scale.append((c, 0.5 * inv[:, V * side : V * side + 1]))
    for j in range(n):
        key = k_ref[at(j), :]
        value = v_ref[at(j), :]
        dv = [None, None]
        dk = [None, None]
        for i in range(j, n):
            query = q_ref[at(i), :]
            g = g_ref[at(i), :]
            dq_part = None
            for side in range(2):
                head = 2 * pair + side
                q_mine = jnp.where(lane // F == head, query * 0.25, 0).astype(BF)
                g_mine = jnp.where(halves[side], g, 0).astype(BF)
                k_mine = jnp.where(lane // F == head, key, 0).astype(BF)
                t = 1.0 + dg(q_mine, key, NT)
                a = t * t + 1.0
                c, inv = scale[2 * i + side]
                ds = (dg(g_mine, value, NT) - c) * inv * t
                if i == j:
                    a = jnp.where(row >= col, a, 0.0)
                    ds = jnp.where(row >= col, ds, 0.0)
                a = a.astype(BF)
                ds = ds.astype(BF)
                x = dg(g_t[V * side : V * side + V, i * blk : (i + 1) * blk], a, NN)
                dv[side] = x if dv[side] is None else dv[side] + x
                x = dg(q_t[pl.ds(pl.multiple_of(F * head, F), F), at(i)], ds, NN)
                dk[side] = x if dk[side] is None else dk[side] + x
                x = dg(ds, k_mine, NN)
                dq_part = x if dq_part is None else dq_part + x
            dq[at(i), :] += dq_part
        lanes = pl.ds(pl.multiple_of(2 * qw + LANES * pair, LANES), LANES)
        out_ref[at(j), lanes] = jnp.concatenate(dv, axis=0).T.astype(BF)
        rows_t = pl.ds(pl.multiple_of(2 * F * pair, 2 * F), 2 * F)
        dk_t[rows_t, at(j)] = jnp.concatenate(dk, axis=0)

    @pl.when(step == pl.num_programs(0) - 1)
    def _():
        out_ref[:, :qw] = dq[...].astype(BF)
        out_ref[:, qw : 2 * qw] = dk_t[...].T.astype(BF)


def attend_bwd(packed, g_own, g_sent, attf, den, me, qw, blk, per, base, pairs, before=None):
    length, width = packed.shape
    skip = 2 * qw // LANES + base
    spec = lambda index, n=length: pl.BlockSpec((n, LANES), index)
    whole = pl.BlockSpec((length, width), lambda p, m: (0, 0))
    extra = [] if before is None else [before]
    return pl.pallas_call(
        functools.partial(attend_bwd_body, blk, per, qw, base),
        grid_spec=pltpu.PrefetchScalarGridSpec(
            num_scalar_prefetch=1,
            grid=(pairs,),
            in_specs=[
                spec(lambda p, m: (0, 0)),
                spec(lambda p, m: (0, 1)),
                spec(lambda p, m: (0, skip + p)),
                spec(lambda p, m: (0, p), g_own.shape[0]),
                spec(lambda p, m: (0, p), g_sent.shape[0]),
                spec(lambda p, m: (0, p)),
                spec(lambda p, m: (0, p)),
            ]
            + [whole] * len(extra),
            out_specs=whole,
            scratch_shapes=[
                pltpu.VMEM((length, LANES), F32),
                pltpu.VMEM((LANES, length), BF),
                pltpu.VMEM((LANES, length), BF),
                pltpu.VMEM((LANES, length), F32),
                pltpu.VMEM((length, LANES), BF),
            ],
        ),
        out_shape=jax.ShapeDtypeStruct((length, width), BF),
        cost_estimate=COST,
        name="attend_bwd",
    )(me, packed, packed, packed, g_own, g_sent, attf, den, *extra)


def ffn_body(tiles, n_ref, dy_ref, wgu_hbm, wd_hbm, *refs):
    hid_ref, gg_ref, ug_ref, out_ref, ng_ref, wgu_ref, wd_ref, sems = refs[-8:]
    copies = []
    for k, (low, high) in enumerate(tiles):
        part = pl.ds(low, high - low)
        copies.append(
            [
                pltpu.make_async_copy(wgu_hbm.at[0, part], wgu_ref.at[0, part], sems.at[k, 0]),
                pltpu.make_async_copy(wgu_hbm.at[1, part], wgu_ref.at[1, part], sems.at[k, 1]),
                pltpu.make_async_copy(wd_hbm.at[part], wd_ref.at[part], sems.at[k, 2]),
            ]
        )
        for copy in copies[-1]:
            copy.start()
    rows = n_ref[...]
    dy = dy_ref[...]
    out = None
    back = None
    for k, (low, high) in enumerate(tiles):
        for copy in copies[k]:
            copy.wait()
        w_gate = wgu_ref[0, low:high, :]
        w_up = wgu_ref[1, low:high, :]
        w_down = wd_ref[low:high, :]
        gate = dg(rows, w_gate, NT)
        upward = dg(rows, w_up, NT)
        hidden_grad = dg(dy, w_down, NT).astype(BF).astype(F32)
        sigma = 1.0 / (1.0 + jnp.exp(-gate))
        swish = gate * sigma
        hidden = (swish * upward).astype(BF)
        gate_grad = (hidden_grad * upward * sigma * (1.0 + gate * (1.0 - sigma))).astype(BF)
        up_grad = (hidden_grad * swish).astype(BF)
        hid_ref[:, low:high] = hidden
        gg_ref[:, low:high] = gate_grad
        ug_ref[:, low:high] = up_grad
        x = dg(hidden, w_down, NN)
        out = x if out is None else out + x
        x = dg(gate_grad, w_gate, NN) + dg(up_grad, w_up, NN)
        back = x if back is None else back + x
    out_ref[...] = out.astype(out_ref.dtype)
    ng_ref[...] = back.astype(ng_ref.dtype)


def ffn(start, total, n_rows, dy_rows, dy_start, w_gate_up, w_down, buffers, kind):
    model = w_down.shape[1]
    width = w_down.shape[0]
    rows = n_rows.shape[0]
    tiles = [(low, min(low + 512, width)) for low in range(0, width, 512)]
    whole = pl.BlockSpec((rows, model), lambda i: (0, 0))
    buffer_spec = pl.BlockSpec((rows, width), lambda i: (start // rows, 0))
    anywhere = pl.BlockSpec(memory_space=pl.ANY)
    extra = [] if buffers is None else list(buffers)
    return pl.pallas_call(
        functools.partial(ffn_body, tiles),
        grid=(1,),
        in_specs=[whole, pl.BlockSpec((rows, model), lambda i: (dy_start // rows, 0)), anywhere, anywhere]
        + [anywhere] * len(extra),
        out_specs=[buffer_spec] * 3 + [whole] * 2,
        out_shape=[jax.ShapeDtypeStruct((total, width), BF)] * 3
        + [jax.ShapeDtypeStruct((rows, model), kind)] * 2,
        scratch_shapes=[
            pltpu.VMEM(w_gate_up.shape, BF),
            pltpu.VMEM(w_down.shape, BF),
            pltpu.SemaphoreType.DMA((len(tiles), 3)),
        ],
        input_output_aliases={} if buffers is None else {4: 0, 5: 1, 6: 2},
        cost_estimate=COST,
        name="ffn",
    )(n_rows, dy_rows, w_gate_up, w_down, *extra)


def wgrad_body(count, core_ref, lhs_ref, *refs):
    rhs_refs = refs[:count]
    keep_ref, send_ref, rhs = refs[count:]

    @pl.when(pl.program_id(0) == 0)
    def _():
        at = 0
        for ref in rhs_refs:
            rhs[at : at + ref.shape[0], :] = ref[...]
            at += ref.shape[0]

    x = dg(lhs_ref[...], rhs[...], TN).astype(BF)
    half = x.shape[1] // 2
    first = core_ref[0] == 0
    keep_ref[...] = jnp.where(first, x[:, :half], x[:, half:])
    send_ref[...] = jnp.where(first, x[:, half:], x[:, :half])


def wgrad(lhs, rhs, core, tile=512):
    rows, width = lhs.shape
    cols = rhs[0].shape[1]
    tile = min(tile, width)
    return pl.pallas_call(
        functools.partial(wgrad_body, len(rhs)),
        grid_spec=pltpu.PrefetchScalarGridSpec(
            num_scalar_prefetch=1,
            grid=(-(-width // tile),),
            in_specs=[pl.BlockSpec((rows, tile), lambda i, s: (0, i))]
            + [pl.BlockSpec(r.shape, lambda i, s: (0, 0)) for r in rhs],
            out_specs=[pl.BlockSpec((tile, cols // 2), lambda i, s: (i, 0))] * 2,
            scratch_shapes=[pltpu.VMEM((rows, cols), BF)],
        ),
        out_shape=[jax.ShapeDtypeStruct((width, cols // 2), BF)] * 2,
        cost_estimate=COST,
        name="wgrad",
    )(core, lhs, *rhs)


def wgrad_pair_body(count, gg_ref, ug_ref, *refs):
    rhs_refs = refs[:count]
    out_ref, rhs = refs[-2:]
    plane = pl.program_id(0)

    @pl.when((plane == 0) & (pl.program_id(1) == 0))
    def _():
        at = 0
        for ref in rhs_refs:
            rhs[at : at + ref.shape[0], :] = ref[...]
            at += ref.shape[0]

    for k, ref in enumerate((gg_ref, ug_ref)):

        @pl.when(plane == k)
        def _(ref=ref):
            out_ref[...] = dg(ref[...], rhs[...], TN).astype(BF)


def wgrad_pair(gate_grad, up_grad, normed2, *others, tile=512):
    rows, width = gate_grad.shape
    cols = normed2[0].shape[1]
    tile = min(tile, width)
    last = -(-width // tile) - 1
    return pl.pallas_call(
        functools.partial(wgrad_pair_body, len(normed2)),
        grid=(2, last + 1),
        in_specs=[
            pl.BlockSpec((rows, tile), lambda p, i: (0, jnp.where(p == 0, i, last))),
            pl.BlockSpec((rows, tile), lambda p, i: (0, jnp.where(p == 0, 0, i))),
        ]
        + [pl.BlockSpec(r.shape, lambda p, i: (0, 0)) for r in normed2]
        + [pl.BlockSpec(memory_space=pl.ANY) for _ in others],
        out_specs=pl.BlockSpec((None, tile, cols), lambda p, i: (p, i, 0)),
        out_shape=jax.ShapeDtypeStruct((2, width, cols), BF),
        scratch_shapes=[pltpu.VMEM((rows, cols), BF)],
        cost_estimate=COST,
        name="wgrad_pair",
    )(gate_grad, up_grad, *normed2, *others)


def wgrad_out_body(count, core_ref, right_ref, *refs):
    keep_ref, send_ref = refs[count:]
    right = right_ref[...]
    first = core_ref[0] == 0
    at = 0
    for ref in refs[:count]:
        x = dg(ref[...], right, TN).astype(BF)
        rows, half = x.shape[0], x.shape[1] // 2
        keep_ref[at : at + rows, :] = jnp.where(first, x[:, :half], x[:, half:])
        send_ref[at : at + rows, :] = jnp.where(first, x[:, half:], x[:, :half])
        at += rows


def wgrad_out(lefts, right, core):
    rows, cols = sum(x.shape[1] for x in lefts), right.shape[1]
    vmem = pl.BlockSpec(memory_space=pltpu.VMEM)
    return pl.pallas_call(
        functools.partial(wgrad_out_body, len(lefts)),
        in_specs=[pl.BlockSpec(memory_space=pltpu.SMEM)] + [vmem] * (1 + len(lefts)),
        out_specs=[vmem] * 2,
        out_shape=[jax.ShapeDtypeStruct((rows, cols // 2), BF)] * 2,
        cost_estimate=COST,
        name="wgrad_out",
    )(core, right, *lefts)


def small_call(body, name, outs, scalar, *arrays):
    vmem = pl.BlockSpec(memory_space=pltpu.VMEM)
    return pl.pallas_call(
        body,
        in_specs=[pl.BlockSpec(memory_space=pltpu.SMEM)] + [vmem] * len(arrays),
        out_specs=[vmem] * len(outs),
        out_shape=[jax.ShapeDtypeStruct(s, t) for s, t in outs],
        cost_estimate=SMALL,
        name=name,
    )(scalar, *arrays)


def add(x, y):
    return (x.astype(F32) + y.astype(F32)).astype(BF)


class Sums:
    def __init__(self):
        self.count = lax.axis_size("dp")
        self.bits = self.count.bit_length() - 1
        self.index = lax.axis_index("dp").astype(jnp.int32)

    def bit(self, b):
        return (self.index >> b) & 1

    def swap(self, x, b):
        return lax.ppermute(x, "dp", [(i, i ^ (1 << b)) for i in range(self.count)])

    def halves(self, x, b, axis):
        half = x.shape[axis] // 2
        low = self.bit(b) * half
        keep = lax.dynamic_slice_in_dim(x, low, half, axis)
        return keep, lax.dynamic_slice_in_dim(x, half - low, half, axis)

    def join(self, mine, got, b, axis):
        low = self.bit(b) == 0
        parts = [jnp.where(low, mine, got), jnp.where(low, got, mine)]
        return jnp.concatenate(parts, axis=axis)


class Order:
    def __init__(self):
        self.last = ()

    def __call__(self, function, *args):
        args, _ = lax.optimization_barrier((args, self.last))
        out = function(*args)
        self.last = tuple(jax.tree.leaves(out))
        return out

    def here(self, x):
        return after(x, *self.last)


class Total:
    def __init__(self, sums, do, halves, bits, axes, finish, also=None):
        self.sums, self.do, self.bits, self.axes = sums, do, bits, axes
        self.finish, self.also = finish, also
        self.x, send = halves
        self.flight = sums.swap(send, 0)
        self.stage = 0

    def step(self):
        sums, (b0, b1, b2), (a0, a1) = self.sums, self.bits, self.axes
        stage = self.stage
        self.stage += 1
        if stage < 2:
            b, axis = ((b0, a0), (b1, a1))[stage]

            def scatter(x, got, *more):
                if more:
                    x = self.also(add(x, got), *more)
                    return sums.halves(x, b, axis)
                x, got = sums.halves(x, b, axis), sums.halves(got, b, axis)
                return add(x[0], got[0]), add(x[1], got[1])

            more = self.also.more() if self.also and stage == 0 else ()
            self.x, send = self.do(scatter, self.x, self.flight, *more)
            self.flight = sums.swap(send, b)
        elif stage < 4:
            self.x = self.do(add, self.x, self.flight)
            self.flight = sums.swap(self.x, b2 if stage == 2 else b1)
        elif stage == 4:
            self.x = self.do(lambda x, got: sums.join(x, got, b1, a1), self.x, self.flight)
            self.flight = sums.swap(self.x, b0)
            self.other = sums.swap(self.x, 0)
        elif stage == 5:
            self.y = self.do.here(self.flight)
            self.do.last = (*self.do.last, self.y)
            self.flight = sums.swap(self.y, 0)
        else:
            self.result = self.do(
                lambda got, other, x, y: self.finish(x, y, other, got),
                self.flight, self.other, self.x, self.y,
            )
            return []
        return [self]


class Beside:
    def __init__(self):
        self.array = None

    def more(self):
        return (self.array,)

    def __call__(self, x, y):
        return jnp.concatenate([x, y], axis=1)


def place_body(plane, count, s_ref, *refs):
    parts, out_ref, wide, sems = refs[:count], refs[-3], refs[-2], refs[-1]
    out = out_ref if plane is None else out_ref.at[plane]
    quarter = wide.shape[2]
    copies = []
    for k, part in enumerate(parts):
        wide[k] = part[...].astype(F32)
        at = ((k >> 1) ^ s_ref[0]) * 2 + ((k & 1) ^ s_ref[1])
        columns = pl.ds(pl.multiple_of(at * quarter, quarter), quarter)
        copies.append(pltpu.make_async_copy(wide.at[k], out.at[:, columns], sems.at[k]))
        copies[-1].start()
    for copy in copies:
        copy.wait()


def place(where, parts, planes=None, plane=None, before=None):
    rows, quarter = parts[0].shape
    shape = (rows, 4 * quarter) if planes is None else (planes, rows, 4 * quarter)
    extra = [] if before is None else [before]
    anywhere = pl.BlockSpec(memory_space=pl.ANY)
    return pl.pallas_call(
        functools.partial(place_body, plane, len(parts)),
        in_specs=[pl.BlockSpec(memory_space=pltpu.SMEM)]
        + [pl.BlockSpec(memory_space=pltpu.VMEM)] * 4
        + [anywhere] * len(extra),
        out_specs=anywhere,
        out_shape=jax.ShapeDtypeStruct(shape, F32),
        scratch_shapes=[pltpu.VMEM((4, rows, quarter), F32), pltpu.SemaphoreType.DMA((4,))],
        input_output_aliases={5: 0} if extra else {},
        cost_estimate=COST,
        name="place",
    )(where, *parts, *extra)


def project_body(x_ref, gain_ref, w_ref, *refs):
    normed_ref, packed_ref = refs[-2:]
    x = x_ref[...].astype(F32)
    normed = (x * scale_of(x) * gain_ref[...]).astype(BF)
    normed_ref[...] = normed
    packed_ref[...] = dg(normed, w_ref[...], NN).astype(BF)


def project(slot, slots, x, gain, w, buffers):
    rows, model = x.shape
    cols = w.shape[1]
    blk = min(256, rows)
    steps = rows // blk
    extra = [] if buffers is None else list(buffers)
    at = lambda c: pl.BlockSpec((blk, c), lambda i: (slot * steps + i, 0))
    full = lambda s: pl.BlockSpec(s, lambda i: (0, 0))
    return pl.pallas_call(
        project_body,
        grid=(steps,),
        in_specs=[pl.BlockSpec((blk, model), lambda i: (i, 0)), full((1, model)), full(w.shape)]
        + [pl.BlockSpec(memory_space=pl.ANY)] * len(extra),
        out_specs=[at(model), at(cols)],
        out_shape=[
            jax.ShapeDtypeStruct((slots * rows, model), BF),
            jax.ShapeDtypeStruct((slots * rows, cols), BF),
        ],
        input_output_aliases={3: 0, 4: 1} if extra else {},
        cost_estimate=COST,
        name="project",
    )(x, gain.reshape(1, model), w, *extra)


def assemble_body(s_ref, *refs):
    out_ref = refs[-1]
    rows = refs[0].shape[0]
    for k, ref in enumerate(refs[:-1]):
        at = ((s_ref[0] ^ (k & 1)) * 2 + (s_ref[1] ^ (k >> 1))) * rows
        out_ref[pl.ds(pl.multiple_of(at, rows), rows), :] = ref[...]


def assemble(where, *pieces):
    rows, cols = pieces[0].shape
    return small_call(assemble_body, "assemble", [((4 * rows, cols), BF)], where, *pieces)[0]


def mix_body(parts, steps, x_ref, *refs):
    resid = x_ref[...].astype(F32)
    for part, weight in zip(refs[:parts], refs[parts : 2 * parts]):
        resid = resid + dg(part[...], weight[...], NN)
    refs = refs[2 * parts :]
    if steps == 0:
        refs[0][...] = resid
        return
    gain_ref, resid_ref, normed_ref = refs[:3]
    resid_ref[...] = resid
    normed = (resid * scale_of(resid) * gain_ref[...]).astype(BF)
    normed_ref[...] = normed
    for k, ref in enumerate(refs[3:]):

        @pl.when(pl.program_id(0) == k)
        def _(ref=ref):
            ref[...] = normed


def part_of(w, k, n):
    return pl.BlockSpec((n, w.shape[1]), lambda i: (k, 0))


def mix(blk, x, parts, weights, gain=None):
    rows, model = x.shape
    at = lambda c: pl.BlockSpec((blk, c), lambda i: (i, 0))
    full = lambda s: pl.BlockSpec(s, lambda i: (0, 0))
    steps = rows // blk
    shape = lambda n, t: jax.ShapeDtypeStruct((n, model), t)
    norm = gain is not None
    out = pl.pallas_call(
        functools.partial(mix_body, len(parts), steps if norm else 0),
        grid=(steps,),
        in_specs=[at(model)]
        + [at(p.shape[1]) for p in parts]
        + [part_of(w, k, n) for w, k, n in weights]
        + ([full((1, model))] if norm else []),
        out_specs=[at(model)] + ([at(model)] + [full((blk, model))] * steps if norm else []),
        out_shape=[shape(rows, F32)] + ([shape(rows, BF)] + [shape(blk, BF)] * steps if norm else []),
        cost_estimate=COST,
        name="mix",
    )(x, *parts, *[w for w, _, _ in weights], *([gain.reshape(1, model)] if norm else []))
    return (out[0], out[1], out[2:]) if norm else out[0]


def turn_body(parts, steps, weights, dy_ref, resid_ref, gain_ref, first_ref, *refs):
    rest, w_refs = refs[:parts], refs[parts : parts + weights]
    grad_ref, mixer_ref, gain_grad_ref = refs[parts + weights : parts + weights + 3]
    g_refs = refs[parts + weights + 3 :]
    grad = first_ref[...]
    for at in range(0, parts, steps):
        x = rest[at][...]
        for k in range(1, steps):
            x = jnp.where(pl.program_id(0) == k, rest[at + k][...], x)
        grad = grad + x.astype(F32)
    back, gain_grad = rms_back(resid_ref[...], gain_ref[...], grad)
    resid_grad = dy_ref[...].astype(F32) + back
    grad_ref[...] = resid_grad
    mixer = resid_grad.astype(BF)
    mixer_ref[...] = mixer
    gain_grad = jnp.sum(gain_grad.reshape(-1, 8, gain_grad.shape[-1]), axis=0)

    @pl.when(pl.program_id(0) == 0)
    def _():
        gain_grad_ref[...] = gain_grad

    @pl.when(pl.program_id(0) > 0)
    def _():
        gain_grad_ref[...] += gain_grad

    for w_ref, g_ref in zip(w_refs, g_refs):
        g_ref[...] = dg(mixer, w_ref[...], NT).astype(BF)


def turn(dy, resid, gain, first, rest, weights):
    rows, model = dy.shape
    blk = rest[0][0].shape[0]
    steps = rows // blk
    at = lambda c: pl.BlockSpec((blk, c), lambda i: (i, 0))
    full = lambda s: pl.BlockSpec(s, lambda i: (0, 0))
    rest = [x for r in rest for x in r]
    return pl.pallas_call(
        functools.partial(turn_body, len(rest), steps, len(weights)),
        grid=(steps,),
        in_specs=[at(model), at(model), full((1, model)), at(model)]
        + [full((blk, model)) for _ in rest]
        + [part_of(w, k, n) for w, k, n in weights],
        out_specs=[at(model), at(model), full((8, model))] + [at(n) for _, _, n in weights],
        out_shape=[
            jax.ShapeDtypeStruct((rows, model), F32),
            jax.ShapeDtypeStruct((rows, model), BF),
            jax.ShapeDtypeStruct((8, model), F32),
        ]
        + [jax.ShapeDtypeStruct((rows, n), BF) for _, _, n in weights],
        cost_estimate=COST,
        name="turn",
    )(dy, resid, gain.reshape(1, model), first, *rest, *[w for w, _, _ in weights])


def scale_of(rows):
    return lax.rsqrt(jnp.mean(rows * rows, axis=-1, keepdims=True) + EPSILON)


def rms_back(rows, gain, grad):
    r = scale_of(rows)
    n = rows * r
    scaled = grad * gain
    back = r * (scaled - n * jnp.mean(scaled * n, axis=-1, keepdims=True))
    return back, grad * n


def order_matrix(heads, qw):
    width = 2 * F + V
    src = lax.broadcasted_iota(jnp.int32, (heads * width, 2 * qw + heads * V), 0)
    dst = lax.broadcasted_iota(jnp.int32, (heads * width, 2 * qw + heads * V), 1)
    head, part = src // width, src % width
    target = jnp.where(
        part < F,
        head * F + part,
        jnp.where(part < 2 * F, qw + head * F + part - F, 2 * qw + head * V + part - 2 * F),
    )
    return (target == dst).astype(BF)


def per_device(
    tokens, norm1_gain, w_qkv, w_out, norm2_gain, w_gate_up, w_down, cotangent, old_mean, momentum
):
    rows, model = tokens.shape
    group = lax.axis_size("tensor")
    length = rows * group
    heads = w_qkv.shape[1] // (2 * F + V)
    hidden_units = w_down.shape[0]
    qw = -(-heads * F // LANES) * LANES
    me = lax.axis_index("tensor")
    me_arr = me.astype(jnp.int32).reshape(1)
    blk = min(256, rows)
    per = rows // blk
    sums = Sums()

    def swap(x, r):
        return lax.ppermute(x, "tensor", [(i, i ^ r) for i in range(group)])

    fast = group == 2 and sums.bits == 4 and heads * V == model // 2 and hidden_units % 32 == 0
    core, y_bit, z_bit = sums.bit(0), sums.bit(1), sums.bit(2)
    core_arr = core.reshape(1)
    others = range(1, group)
    do = Order()
    step = max(rows // 2, 128)
    cuts = range(0, rows, step)

    arrived = [swap(tokens, r) for r in others]
    order = order_matrix(heads, qw)
    w_ordered = do(lambda w: dg(w, order, NN).astype(BF), w_qkv)
    quarter = w_out.shape[0] // 4
    buffers = do(lambda x, w: project(0, group, x, norm1_gain, w, None), tokens, w_ordered)
    upstream = {(0, 0): cotangent}

    def cut_inputs(dy, w, *_):
        low = (2 * y_bit + core) * quarter
        piece = lax.dynamic_slice_in_dim(w, low, quarter, 0) if fast else w
        return piece, [dy[low : low + step] for low in cuts]

    w_piece, dy_cuts = do(cut_inputs, cotangent, w_out, *arrived)
    if fast:
        piece = swap(w_piece, 1)
    else:
        w_rest = [swap(w_out, r) for r in others]
    for r in others:
        upstream[r, 0] = swap(dy_cuts[0], r)
    for r in others:
        buffers = do(
            lambda x, *b, r=r: project(r, group, x, norm1_gain, w_ordered, b), arrived[r - 1], *buffers
        )
    normed, packed = buffers

    pairs = heads // 2
    groups = 2 if pairs % 2 == 0 else 1
    each = pairs // groups
    span = each * LANES
    attended, crossed = [], []
    for k in range(groups):
        attended.append(
            do(lambda x, k=k: attend_fwd(x, me_arr, heads, qw, blk, per, k * each, each), packed)
        )
        for r in others:
            crossed.append((k, r, swap(attended[k][1][(r - 1) * rows : r * rows], r)))
        if fast and k == 0:
            piece = do.here(piece)
            piece_y = sums.swap(piece, 1)
            piece_core = sums.swap(piece, 0)
    att_own, att_sent, attf, den, den_sum = zip(*attended)
    upstream_first = do.here(tuple(upstream[r, 0] for r in others))
    do.last = (*do.last, *upstream_first)
    if fast:
        piece_y = do.here(piece_y)
        piece_both = sums.swap(piece_y, 0)
        place_of = jnp.stack([y_bit, core])
        w_rest, _ = do(
            lambda c, x, y, p, q: (assemble(place_of, p, q, x, y), c),
            [x for k, _, x in crossed if k == 0], piece_core, piece_both, piece, piece_y,
        )
        w_rest = [w_rest]

    parts = list(att_own) + [x for _, _, x in crossed]
    blocks_of = [(0, k) for k in range(groups)] + [(r, k) for k, r, _ in crossed]
    with_blocks = lambda ws, at: [(ws[r], k, span) for r, k in at]
    for low, dy_cut in zip(cuts[1:], dy_cuts[1:]):
        for r in others:
            upstream[r, low] = swap(do.here(after(dy_cut, *parts)), r)
    resid, own2, own2_cuts = do(
        lambda x, w: mix(step, tokens, x, with_blocks(w, blocks_of), norm2_gain),
        parts, [w_out, *w_rest],
    )

    w_gate_up = jnp.swapaxes(w_gate_up, 1, 2)
    blocks = [(0, 0)] + [(r, low) for r in others for low in cuts]
    normed2, waiting = [own2], own2
    buffers = ()
    out_parts, back_parts = [], []
    for at, (r, low) in enumerate(blocks):
        if r > 0:
            x = own2_cuts[low // step]
            normed2.append(swap(x if at == 1 else after(x, waiting), r))
        kind = F32 if r == 0 else BF
        taken = [dy for (q, _), dy in upstream.items() if q > 0] if at == 1 else []
        *buffers, out_part, back_part = do(
            lambda x, dy, b, t, r=r, low=low, kind=kind: ffn(
                r * rows + low, length, x, dy, 0, w_gate_up, w_down, b or None, kind
            ),
            normed2[-1],
            upstream[r, low],
            buffers,
            taken,
        )
        if at == 0:
            waiting, first_out, first_back = out_part, out_part, back_part
        else:
            out_parts.append((out_part, r))
            back_parts.append((r, low, swap(back_part, r)))
    hidden, gate_grad, up_grad = buffers
    dy_all = [upstream[k] for k in blocks]
    back_parts = [[x for q, _, x in back_parts if q == r] for r in others]

    def finish_output(resid, first_out, *got):
        output = resid + first_out
        got = got[::-1]
        for r in others:
            count = len(cuts)
            part = got[(r - 1) * count : r * count]
            output = output + jnp.concatenate(part, axis=0).astype(F32)
        return output.astype(BF)

    def finish_norm1(p, resid_grad, *got):
        grad = dg(p[:rows], w_ordered, NT)
        for x in got:
            grad = grad + x.astype(F32)
        back, gain_grad = rms_back(tokens.astype(F32), norm1_gain, grad)
        return resid_grad + back, jnp.sum(gain_grad, axis=0)

    def halve(x, got):
        half = x.shape[0] // 2
        return add(x[:half], got[:half]), add(x[half:], got[half:])

    def qkv_halves(normed, packed_grad):
        keep, send = sums.halves(normed, 0, 1)
        return dg(keep, packed_grad, TN).astype(BF), dg(send, packed_grad, TN).astype(BF)

    def both(x, y, x_other, y_other):
        mine, theirs = sums.join(x, y, 1, 0), sums.join(x_other, y_other, 1, 0)
        cols = packed.shape[1]
        qkv = sums.join(mine[:, :cols], theirs[:, :cols], 0, 0)
        out = sums.join(mine[:, cols:], theirs[:, cols:], 0, 1)
        return dg(qkv, order, NT), out.astype(F32)

    links = [lambda x, r=r: swap(x, 1 << r) for r in range(group.bit_length() - 1)]
    links += [lambda x, b=b: sums.swap(x, b) for b in range(sums.bits)]
    by_y, by_z = jnp.stack([core, y_bit]), jnp.stack([core, z_bit])
    wgrad_of = lambda x, r, *_: wgrad(x, r, core_arr)
    beside = Beside()
    now = {"bwd": 0, "packed_grad": None, "w": 0, "link": 0}
    chains = {}

    def make_gate():
        halves = do(wgrad_of, gate_grad, normed2)
        finish = lambda *x: place(by_y, x, 2, 0, now.get("pair"))
        chains["G"] = Total(sums, do, halves, (1, 2, 3), (1, 1), finish)

    def make_up():
        halves = do(wgrad_of, up_grad, normed2, [x[0] for x in back_parts])
        finish = lambda *x: place(by_y, x, 2, 1, now.get("pair"))
        chains["U"] = Total(sums, do, halves, (1, 2, 3), (1, 1), finish)

    def make_down():
        halves = do(wgrad_of, hidden, dy_all)
        chains["D"] = Total(sums, do, halves, (2, 1, 3), (1, 1), lambda *x: place(by_z, x))

    def make_qkv():
        halves = do(qkv_halves, normed, now["packed_grad"])
        chains["Q"] = Total(sums, do, halves, (1, 2, 3), (0, 0), both, beside)

    def step_of(name):
        def step():
            chains[name].step()
            if name in "GU" and chains[name].stage == 7:
                now["pair"] = chains[name].result

        return step

    def turn_rows():
        turned = [(r, k) for r in range(group) for k in range(groups)]
        now["resid_grad"], now["mixer"], now["gain2"], *g_all = do(
            lambda *x: turn(*x[:2], norm2_gain, x[2], x[3], with_blocks(x[4], turned)),
            cotangent, resid, first_back, back_parts, [w_out, *w_rest],
        )
        now["g_own"], now["g_sent"] = g_all[:groups], []
        for k in range(groups):
            x = [swap(g_all[r * groups + k], r) for r in others]
            now["g_sent"].append(x[0] if group == 2 else jnp.concatenate(x, axis=0))

    def make_out():
        now["wx"], send = do(
            lambda m, p, *_: wgrad_out(p, m, core_arr), now["mixer"], parts, *reversed(now["g_sent"])
        )
        now["w_flight"] = sums.swap(send, 0)

    def step_out():
        now["w"] += 1
        if now["w"] == 1:
            now["wx"], send = do(halve, now["wx"], now["w_flight"])
            now["w_flight"] = swap(send, 1)
        else:
            beside.array = do(add, now["wx"], now["w_flight"])

    def backward():
        k = now["bwd"]
        now["bwd"] += 1
        before = [] if k == 0 else [now["packed_grad"]]
        now["packed_grad"] = do(
            lambda g, s, f, d, *b: attend_bwd(
                packed, g, s, f, d, me_arr, qw, blk, per, k * each, each, *b
            ),
            now["g_own"][k], now["g_sent"][k], attf[k], den[k], *before,
        )

    def send_tokens():
        now["back1"] = []
        for r in others:
            part = do(
                lambda p, r=r: dg(p[r * rows : (r + 1) * rows], w_ordered, NT).astype(BF),
                now["packed_grad"],
            )
            now["back1"].append(swap(part, r))

    def finish_tokens():
        now["input_grad"], gain1_grad = do(
            finish_norm1, now["packed_grad"], now["resid_grad"], *now["back1"]
        )
        denom_local = sum(jnp.sum(d) for d in den_sum) * (0.5 / V)
        small = jnp.concatenate(
            [gain1_grad, jnp.sum(now["gain2"], axis=0), jnp.full((model,), denom_local / model)]
        )
        now["small"] = small.reshape(3 * model // LANES, LANES)
        now["flight"] = links[0](now["small"])

    def step_small():
        now["small"] = do(lambda x, y: x + y, now["small"], now["flight"])
        now["link"] += 1
        if now["link"] < len(links):
            now["flight"] = links[now["link"]](now["small"])

    def send_rows():
        now["got_out"] = [swap(do.here(x), k) for x, k in out_parts]

    def finish_rows():
        now["output"] = do(finish_output, resid, first_out, *reversed(now["got_out"]))

    steps = dict(
        g=make_gate, u=make_up, d=make_down, q=make_qkv, t=turn_rows, w=make_out, W=step_out,
        A=backward, K=send_tokens, N=finish_tokens, s=step_small, O=send_rows, o=finish_rows,
        G=step_of("G"), U=step_of("U"), D=step_of("D"), Q=step_of("Q"),
    )
    for name in FAST if fast else "t" + "A" * groups + "KNOo" + "s" * len(links):
        steps[name]()
    input_grad, output, mixer_own = now["input_grad"], now["output"], now["mixer"]
    packed_grad = now["packed_grad"]
    small = now["small"].reshape(3, model)
    denom_total = jnp.sum(small[2])

    if fast:
        grad_gate_up, grad_down = now["pair"], chains["D"].result
        grad_qkv, grad_out = chains["Q"].result
    else:
        mixer_grad = jnp.concatenate([mixer_own] + [swap(mixer_own, r) for r in others], axis=0)
        att = jnp.concatenate(
            [jnp.concatenate(att_own, axis=1), jnp.concatenate(att_sent, axis=1)], axis=0
        )
        all_normed2 = jnp.concatenate(normed2, axis=0)
        all_upstream = jnp.concatenate(dy_all, axis=0)
        grad_down = dg(hidden, all_upstream, TN)
        grad_gate = dg(gate_grad, all_normed2, TN)
        grad_up = dg(up_grad, all_normed2, TN)
        grad_out = dg(att, mixer_grad, TN)
        grad_qkv = dg(dg(normed, packed_grad, TN).astype(BF), order, NT)
        grad_qkv, grad_out, grad_gate, grad_up, grad_down = lax.psum(
            (grad_qkv, grad_out, grad_gate, grad_up, grad_down), "dp"
        )
        grad_gate_up = jnp.stack([grad_gate, grad_up])
    grad_gate_up = jnp.swapaxes(grad_gate_up, 1, 2)

    rows_all = length * lax.axis_size("dp")
    per_row = heads * group * length
    mean_value = denom_total / rows_all / per_row
    new_mean = momentum * old_mean + (1.0 - momentum) * mean_value
    return (
        output,
        input_grad,
        small[0],
        grad_qkv,
        grad_out,
        small[1],
        grad_gate_up,
        grad_down,
        new_mean,
    )


def solution(mesh):
    rows = P(("dp", "tensor"), None)
    return jax.shard_map(
        per_device,
        mesh=mesh,
        in_specs=(
            rows, P(), P(None, "tensor"), P("tensor", None), P(),
            P(None, None, "tensor"), P("tensor", None), rows, P(), P(),
        ),
        out_specs=(
            rows, rows, P(), P(None, "tensor"), P("tensor", None), P(),
            P(None, None, "tensor"), P("tensor", None), P(),
        ),
        check_vma=False,
    )
```

```python
import functools

import jax
import jax.numpy as jnp
from jax import lax
from jax.experimental import pallas as pl
from jax.experimental.pallas import tpu as pltpu
from jax.sharding import PartitionSpec as P

F = 16
V = 64
EPSILON = 1e-05
F32 = jnp.float32
BF = jnp.bfloat16
NT = (((1,), (1,)), ((), ()))
NN = (((1,), (0,)), ((), ()))
TN = (((0,), (0,)), ((), ()))
LANES = 128
COST = pl.CostEstimate(flops=5 * 10**10, bytes_accessed=10**8, transcendentals=0)
SMALL = COST
FAST = (
    "gtGUDwGAUDWGAKqUDWGQUDG"
    "NOQUDGsoQsQGsUQDsUDQsQ"
)


def after(x, *others):
    return lax.optimization_barrier((x, *others))[0]


def dg(a, b, dims):
    return lax.dot_general(a, b, dims, preferred_element_type=F32)


def attend_fwd_body(blk, per, base, me_ref, q_ref, k_ref, v_ref, own_ref, sent_ref, attf_ref, den_ref, sum_ref, vals, att_s):
    length = q_ref.shape[0]
    n = length // blk
    pair = pl.program_id(0)
    flip = me_ref[0] * per

    def at(b):
        return pl.ds(pl.multiple_of((b ^ flip) * blk, blk), blk)

    vals[:, :LANES] = v_ref[...]
    eights = jnp.zeros((8, LANES), F32)

    @pl.when(pair == 0)
    def _():
        vals[:, LANES:] = jnp.ones((length, LANES), BF)

    lane = lax.broadcasted_iota(jnp.int32, (blk, LANES), 1)
    row = lax.broadcasted_iota(jnp.int32, (blk, blk), 0)
    col = lax.broadcasted_iota(jnp.int32, (blk, blk), 1)
    for i in range(n):
        query = q_ref[at(i), :]
        sums = []
        for side in range(2):
            mine = jnp.where(lane // F == 2 * (base + pair) + side, query * 0.25, 0).astype(BF)
            total = None
            for j in range(i + 1):
                t = 1.0 + dg(mine, k_ref[at(j), :], NT)
                a = t * t + 1.0
                if j == i:
                    a = jnp.where(row >= col, a, 0.0)
                part = dg(a.astype(BF), vals[at(j), :], NN)
                total = part if total is None else total + part
            sums.append(total)
        numer = jnp.where(lane < V, sums[0][:, :LANES], sums[1][:, :LANES])
        denom = jnp.where(lane < V, sums[0][:, LANES:], sums[1][:, LANES:])
        att = numer / denom
        att_s[at(i), :] = att.astype(BF)
        attf_ref[at(i), :] = att
        den_ref[at(i), :] = denom
        eights = eights + jnp.sum(denom.reshape(-1, 8, LANES), axis=0)
    sum_ref[...] = eights
    rows = own_ref.shape[0]
    own_ref[...] = att_s[:rows, :]
    sent_ref[...] = att_s[rows:, :]


def attend_fwd(packed, me, heads, qw, blk, per, base, pairs):
    length = packed.shape[0]
    rows = blk * per
    skip = 2 * qw // LANES + base
    spec = lambda index, n=length: pl.BlockSpec((n, LANES), index)
    column = lambda p, m: (0, p)
    width = LANES * pairs
    return pl.pallas_call(
        functools.partial(attend_fwd_body, blk, per, base),
        grid_spec=pltpu.PrefetchScalarGridSpec(
            num_scalar_prefetch=1,
            grid=(pairs,),
            in_specs=[
                spec(lambda p, m: (0, 0)),
                spec(lambda p, m: (0, 1)),
                spec(lambda p, m: (0, skip + p)),
            ],
            out_specs=[
                spec(column, rows),
                spec(column, length - rows),
                spec(column),
                spec(column),
                spec(column, 8),
            ],
            scratch_shapes=[pltpu.VMEM((length, 2 * LANES), BF), pltpu.VMEM((length, LANES), BF)],
        ),
        out_shape=[
            jax.ShapeDtypeStruct((rows, width), BF),
            jax.ShapeDtypeStruct((length - rows, width), BF),
            jax.ShapeDtypeStruct((length, width), F32),
            jax.ShapeDtypeStruct((length, width), F32),
            jax.ShapeDtypeStruct((8, width), F32),
        ],
        cost_estimate=COST,
        name="attend_fwd",
    )(me, packed, packed, packed)


def attend_bwd_body(blk, per, qw, base, me_ref, q_ref, k_ref, v_ref, g_own, g_sent, attf_ref, den_ref, *refs):
    out_ref, dq, q_t, g_t, dk_t, g_ref = refs[-6:]
    length = q_ref.shape[0]
    n = length // blk
    step = pl.program_id(0)
    pair = base + step
    flip = me_ref[0] * per

    def at(b):
        return pl.ds(pl.multiple_of((b ^ flip) * blk, blk), blk)

    lane = lax.broadcasted_iota(jnp.int32, (blk, LANES), 1)
    row = lax.broadcasted_iota(jnp.int32, (blk, blk), 0)
    col = lax.broadcasted_iota(jnp.int32, (blk, blk), 1)
    halves = (lane < V, lane >= V)

    @pl.when(step == 0)
    def _():
        q_t[...] = q_ref[...].T
        if base == 0:
            dq[...] = jnp.zeros_like(dq)
            dk_t[...] = jnp.zeros_like(dk_t)
        else:
            before = refs[0]
            dq[...] = before[:, :qw].astype(F32)
            dk_t[...] = before[:, qw : 2 * qw].astype(F32).T
            done = 2 * qw + LANES * base
            out_ref[:, 2 * qw : done] = before[:, 2 * qw : done]

    rows = g_own.shape[0]
    g_ref[:rows, :] = g_own[...]
    g_ref[rows:, :] = g_sent[...]
    scale = []
    for i in range(n):
        g = g_ref[at(i), :].astype(F32)
        inv = 1.0 / den_ref[at(i), :]
        ga = g * attf_ref[at(i), :]
        g_t[:, i * blk : (i + 1) * blk] = (g * inv).astype(BF).T
        for side in range(2):
            c = jnp.sum(jnp.where(halves[side], ga, 0.0), axis=1, keepdims=True)
            scale.append((c, 0.5 * inv[:, V * side : V * side + 1]))
    for j in range(n):
        key = k_ref[at(j), :]
        value = v_ref[at(j), :]
        dv = [None, None]
        dk = [None, None]
        for i in range(j, n):
            query = q_ref[at(i), :]
            g = g_ref[at(i), :]
            dq_part = None
            for side in range(2):
                head = 2 * pair + side
                q_mine = jnp.where(lane // F == head, query * 0.25, 0).astype(BF)
                g_mine = jnp.where(halves[side], g, 0).astype(BF)
                k_mine = jnp.where(lane // F == head, key, 0).astype(BF)
                t = 1.0 + dg(q_mine, key, NT)
                a = t * t + 1.0
                c, inv = scale[2 * i + side]
                ds = (dg(g_mine, value, NT) - c) * inv * t
                if i == j:
                    a = jnp.where(row >= col, a, 0.0)
                    ds = jnp.where(row >= col, ds, 0.0)
                a = a.astype(BF)
                ds = ds.astype(BF)
                x = dg(g_t[V * side : V * side + V, i * blk : (i + 1) * blk], a, NN)
                dv[side] = x if dv[side] is None else dv[side] + x
                x = dg(q_t[pl.ds(pl.multiple_of(F * head, F), F), at(i)], ds, NN)
                dk[side] = x if dk[side] is None else dk[side] + x
                x = dg(ds, k_mine, NN)
                dq_part = x if dq_part is None else dq_part + x
            dq[at(i), :] += dq_part
        lanes = pl.ds(pl.multiple_of(2 * qw + LANES * pair, LANES), LANES)
        out_ref[at(j), lanes] = jnp.concatenate(dv, axis=0).T.astype(BF)
        rows_t = pl.ds(pl.multiple_of(2 * F * pair, 2 * F), 2 * F)
        dk_t[rows_t, at(j)] = jnp.concatenate(dk, axis=0)

    @pl.when(step == pl.num_programs(0) - 1)
    def _():
        out_ref[:, :qw] = dq[...].astype(BF)
        out_ref[:, qw : 2 * qw] = dk_t[...].T.astype(BF)


def attend_bwd(packed, g_own, g_sent, attf, den, me, qw, blk, per, base, pairs, before=None):
    length, width = packed.shape
    skip = 2 * qw // LANES + base
    spec = lambda index, n=length: pl.BlockSpec((n, LANES), index)
    whole = pl.BlockSpec((length, width), lambda p, m: (0, 0))
    extra = [] if before is None else [before]
    return pl.pallas_call(
        functools.partial(attend_bwd_body, blk, per, qw, base),
        grid_spec=pltpu.PrefetchScalarGridSpec(
            num_scalar_prefetch=1,
            grid=(pairs,),
            in_specs=[
                spec(lambda p, m: (0, 0)),
                spec(lambda p, m: (0, 1)),
                spec(lambda p, m: (0, skip + p)),
                spec(lambda p, m: (0, p), g_own.shape[0]),
                spec(lambda p, m: (0, p), g_sent.shape[0]),
                spec(lambda p, m: (0, p)),
                spec(lambda p, m: (0, p)),
            ]
            + [whole] * len(extra),
            out_specs=whole,
            scratch_shapes=[
                pltpu.VMEM((length, LANES), F32),
                pltpu.VMEM((LANES, length), BF),
                pltpu.VMEM((LANES, length), BF),
                pltpu.VMEM((LANES, length), F32),
                pltpu.VMEM((length, LANES), BF),
            ],
        ),
        out_shape=jax.ShapeDtypeStruct((length, width), BF),
        cost_estimate=COST,
        name="attend_bwd",
    )(me, packed, packed, packed, g_own, g_sent, attf, den, *extra)


def ffn_body(tiles, n_ref, dy_ref, wgu_hbm, wd_hbm, *refs):
    hid_ref, gg_ref, ug_ref, out_ref, ng_ref, wgu_ref, wd_ref, sems = refs[-8:]
    copies = []
    for k, (low, high) in enumerate(tiles):
        part = pl.ds(low, high - low)
        copies.append(
            [
                pltpu.make_async_copy(wgu_hbm.at[0, part], wgu_ref.at[0, part], sems.at[k, 0]),
                pltpu.make_async_copy(wgu_hbm.at[1, part], wgu_ref.at[1, part], sems.at[k, 1]),
                pltpu.make_async_copy(wd_hbm.at[part], wd_ref.at[part], sems.at[k, 2]),
            ]
        )
        for copy in copies[-1]:
            copy.start()
    rows = n_ref[...]
    dy = dy_ref[...]
    out = None
    back = None
    for k, (low, high) in enumerate(tiles):
        for copy in copies[k]:
            copy.wait()
        w_gate = wgu_ref[0, low:high, :]
        w_up = wgu_ref[1, low:high, :]
        w_down = wd_ref[low:high, :]
        gate = dg(rows, w_gate, NT)
        upward = dg(rows, w_up, NT)
        hidden_grad = dg(dy, w_down, NT).astype(BF).astype(F32)
        sigma = 1.0 / (1.0 + jnp.exp(-gate))
        swish = gate * sigma
        hidden = (swish * upward).astype(BF)
        gate_grad = (hidden_grad * upward * sigma * (1.0 + gate * (1.0 - sigma))).astype(BF)
        up_grad = (hidden_grad * swish).astype(BF)
        hid_ref[:, low:high] = hidden
        gg_ref[:, low:high] = gate_grad
        ug_ref[:, low:high] = up_grad
        x = dg(hidden, w_down, NN)
        out = x if out is None else out + x
        x = dg(gate_grad, w_gate, NN) + dg(up_grad, w_up, NN)
        back = x if back is None else back + x
    out_ref[...] = out.astype(out_ref.dtype)
    ng_ref[...] = back.astype(ng_ref.dtype)


def ffn(start, total, n_rows, dy_rows, dy_start, w_gate_up, w_down, buffers, kind):
    model = w_down.shape[1]
    width = w_down.shape[0]
    rows = n_rows.shape[0]
    tiles = [(low, min(low + 512, width)) for low in range(0, width, 512)]
    whole = pl.BlockSpec((rows, model), lambda i: (0, 0))
    buffer_spec = pl.BlockSpec((rows, width), lambda i: (start // rows, 0))
    anywhere = pl.BlockSpec(memory_space=pl.ANY)
    extra = [] if buffers is None else list(buffers)
    return pl.pallas_call(
        functools.partial(ffn_body, tiles),
        grid=(1,),
        in_specs=[whole, pl.BlockSpec((rows, model), lambda i: (dy_start // rows, 0)), anywhere, anywhere]
        + [anywhere] * len(extra),
        out_specs=[buffer_spec] * 3 + [whole] * 2,
        out_shape=[jax.ShapeDtypeStruct((total, width), BF)] * 3
        + [jax.ShapeDtypeStruct((rows, model), kind)] * 2,
        scratch_shapes=[
            pltpu.VMEM(w_gate_up.shape, BF),
            pltpu.VMEM(w_down.shape, BF),
            pltpu.SemaphoreType.DMA((len(tiles), 3)),
        ],
        input_output_aliases={} if buffers is None else {4: 0, 5: 1, 6: 2},
        cost_estimate=COST,
        name="ffn",
    )(n_rows, dy_rows, w_gate_up, w_down, *extra)


def wgrads_body(n_count, y_count, core_ref, *refs):
    lhs_refs, refs = refs[:3], refs[3:]
    n_refs, y_refs, refs = refs[:n_count], refs[n_count : n_count + y_count], refs[n_count + y_count :]
    outs, (n_all, y_all) = refs[-8:-2], refs[-2:]
    plane = pl.program_id(0)
    first = core_ref[0] == 0
    for start, parts, whole in ((0, n_refs, n_all), (2, y_refs, y_all)):

        @pl.when((plane == start) & (pl.program_id(1) == 0))
        def _(parts=parts, whole=whole):
            at = 0
            for ref in parts:
                whole[at : at + ref.shape[0], :] = ref[...]
                at += ref.shape[0]

    for k, (lhs, rhs) in enumerate(zip(lhs_refs, (n_all, n_all, y_all))):

        @pl.when(plane == k)
        def _(k=k, lhs=lhs, rhs=rhs):
            x = dg(lhs[...], rhs[...], TN).astype(BF)
            half = x.shape[1] // 2
            outs[2 * k][...] = jnp.where(first, x[:, :half], x[:, half:])
            outs[2 * k + 1][...] = jnp.where(first, x[:, half:], x[:, :half])


def wgrads(lhs, normed2, upstream, core, *others, tile=512):
    rows, width = lhs[0].shape
    cols = normed2[0].shape[1]
    tile = min(tile, width)
    last = -(-width // tile) - 1

    def walk(k, p, i):
        return jnp.where(p == k, i, jnp.where(p < k, 0, last))

    out = lambda k: pl.BlockSpec((tile, cols // 2), lambda p, i, s: (walk(k, p, i), 0))
    return pl.pallas_call(
        functools.partial(wgrads_body, len(normed2), len(upstream)),
        grid_spec=pltpu.PrefetchScalarGridSpec(
            num_scalar_prefetch=1,
            grid=(3, last + 1),
            in_specs=[
                pl.BlockSpec((rows, tile), lambda p, i, s, k=k: (0, walk(k, p, i))) for k in range(3)
            ]
            + [pl.BlockSpec(r.shape, lambda p, i, s: (0, 0)) for r in (*normed2, *upstream)]
            + [pl.BlockSpec(memory_space=pl.ANY) for _ in others],
            out_specs=[out(k // 2) for k in range(6)],
            scratch_shapes=[pltpu.VMEM((rows, cols), BF)] * 2,
        ),
        out_shape=[jax.ShapeDtypeStruct((width, cols // 2), BF)] * 6,
        cost_estimate=COST,
        name="wgrads",
    )(core, *lhs, *normed2, *upstream, *others)


def wgrad_out_body(count, core_ref, right_ref, *refs):
    keep_ref, send_ref = refs[count:]
    right = right_ref[...]
    first = core_ref[0] == 0
    at = 0
    for ref in refs[:count]:
        x = dg(ref[...], right, TN).astype(BF)
        rows, half = x.shape[0], x.shape[1] // 2
        keep_ref[at : at + rows, :] = jnp.where(first, x[:, :half], x[:, half:])
        send_ref[at : at + rows, :] = jnp.where(first, x[:, half:], x[:, :half])
        at += rows


def wgrad_out(lefts, right, core):
    rows, cols = sum(x.shape[1] for x in lefts), right.shape[1]
    vmem = pl.BlockSpec(memory_space=pltpu.VMEM)
    return pl.pallas_call(
        functools.partial(wgrad_out_body, len(lefts)),
        in_specs=[pl.BlockSpec(memory_space=pltpu.SMEM)] + [vmem] * (1 + len(lefts)),
        out_specs=[vmem] * 2,
        out_shape=[jax.ShapeDtypeStruct((rows, cols // 2), BF)] * 2,
        cost_estimate=COST,
        name="wgrad_out",
    )(core, right, *lefts)


def small_call(body, name, outs, scalar, *arrays):
    vmem = pl.BlockSpec(memory_space=pltpu.VMEM)
    return pl.pallas_call(
        body,
        in_specs=[pl.BlockSpec(memory_space=pltpu.SMEM)] + [vmem] * len(arrays),
        out_specs=[vmem] * len(outs),
        out_shape=[jax.ShapeDtypeStruct(s, t) for s, t in outs],
        cost_estimate=SMALL,
        name=name,
    )(scalar, *arrays)


def add(x, y):
    return (x.astype(F32) + y.astype(F32)).astype(BF)


class Sums:
    def __init__(self):
        self.count = lax.axis_size("dp")
        self.bits = self.count.bit_length() - 1
        self.index = lax.axis_index("dp").astype(jnp.int32)

    def bit(self, b):
        return (self.index >> b) & 1

    def swap(self, x, b):
        return lax.ppermute(x, "dp", [(i, i ^ (1 << b)) for i in range(self.count)])

    def halves(self, x, b, axis):
        half = x.shape[axis] // 2
        low = self.bit(b) * half
        keep = lax.dynamic_slice_in_dim(x, low, half, axis)
        return keep, lax.dynamic_slice_in_dim(x, half - low, half, axis)

    def join(self, mine, got, b, axis):
        low = self.bit(b) == 0
        parts = [jnp.where(low, mine, got), jnp.where(low, got, mine)]
        return jnp.concatenate(parts, axis=axis)


class Order:
    def __init__(self):
        self.last = ()

    def __call__(self, function, *args):
        args, _ = lax.optimization_barrier((args, self.last))
        out = function(*args)
        self.last = tuple(jax.tree.leaves(out))
        return out

    def here(self, x):
        return after(x, *self.last)


class Total:
    def __init__(self, sums, do, halves, bits, axes, finish, also=None):
        self.sums, self.do, self.bits, self.axes = sums, do, bits, axes
        self.finish, self.also = finish, also
        self.x, send = halves
        self.flight = sums.swap(send, 0)
        self.stage = 0

    def step(self):
        sums, (b0, b1, b2), (a0, a1) = self.sums, self.bits, self.axes
        stage = self.stage
        self.stage += 1
        if stage < 2:
            b, axis = ((b0, a0), (b1, a1))[stage]

            def scatter(x, got, *more):
                if more:
                    x = self.also(add(x, got), *more)
                    return sums.halves(x, b, axis)
                x, got = sums.halves(x, b, axis), sums.halves(got, b, axis)
                return add(x[0], got[0]), add(x[1], got[1])

            more = self.also.more() if self.also and stage == 0 else ()
            self.x, send = self.do(scatter, self.x, self.flight, *more)
            self.flight = sums.swap(send, b)
        elif stage < 4:
            self.x = self.do(add, self.x, self.flight)
            self.flight = sums.swap(self.x, b2 if stage == 2 else b1)
        elif stage == 4:
            self.x = self.do(lambda x, got: sums.join(x, got, b1, a1), self.x, self.flight)
            self.flight = sums.swap(self.x, b0)
            self.other = sums.swap(self.x, 0)
        elif stage == 5:
            self.y = self.do.here(self.flight)
            self.do.last = (*self.do.last, self.y)
            self.flight = sums.swap(self.y, 0)
        else:
            self.result = self.do(
                lambda got, other, x, y: self.finish(x, y, other, got),
                self.flight, self.other, self.x, self.y,
            )
            return []
        return [self]


class Beside:
    def __init__(self):
        self.array = None

    def more(self):
        return (self.array,)

    def __call__(self, x, y):
        return jnp.concatenate([x, y], axis=1)


def place_body(plane, count, s_ref, *refs):
    parts, out_ref, wide, sems = refs[:count], refs[-3], refs[-2], refs[-1]
    out = out_ref if plane is None else out_ref.at[plane]
    quarter = wide.shape[2]
    copies = []
    for k, part in enumerate(parts):
        wide[k] = part[...].astype(F32)
        at = ((k >> 1) ^ s_ref[0]) * 2 + ((k & 1) ^ s_ref[1])
        columns = pl.ds(pl.multiple_of(at * quarter, quarter), quarter)
        copies.append(pltpu.make_async_copy(wide.at[k], out.at[:, columns], sems.at[k]))
        copies[-1].start()
    for copy in copies:
        copy.wait()


def place(where, parts, planes=None, plane=None, before=None):
    rows, quarter = parts[0].shape
    shape = (rows, 4 * quarter) if planes is None else (planes, rows, 4 * quarter)
    extra = [] if before is None else [before]
    anywhere = pl.BlockSpec(memory_space=pl.ANY)
    return pl.pallas_call(
        functools.partial(place_body, plane, len(parts)),
        in_specs=[pl.BlockSpec(memory_space=pltpu.SMEM)]
        + [pl.BlockSpec(memory_space=pltpu.VMEM)] * 4
        + [anywhere] * len(extra),
        out_specs=anywhere,
        out_shape=jax.ShapeDtypeStruct(shape, F32),
        scratch_shapes=[pltpu.VMEM((4, rows, quarter), F32), pltpu.SemaphoreType.DMA((4,))],
        input_output_aliases={5: 0} if extra else {},
        cost_estimate=COST,
        name="place",
    )(where, *parts, *extra)


def project_body(x_ref, gain_ref, w_ref, *refs):
    normed_ref, packed_ref = refs[-2:]
    x = x_ref[...].astype(F32)
    normed = (x * scale_of(x) * gain_ref[...]).astype(BF)
    normed_ref[...] = normed
    packed_ref[...] = dg(normed, w_ref[...], NN).astype(BF)


def project(slot, slots, x, gain, w, buffers):
    rows, model = x.shape
    cols = w.shape[1]
    blk = min(256, rows)
    steps = rows // blk
    extra = [] if buffers is None else list(buffers)
    at = lambda c: pl.BlockSpec((blk, c), lambda i: (slot * steps + i, 0))
    full = lambda s: pl.BlockSpec(s, lambda i: (0, 0))
    return pl.pallas_call(
        project_body,
        grid=(steps,),
        in_specs=[pl.BlockSpec((blk, model), lambda i: (i, 0)), full((1, model)), full(w.shape)]
        + [pl.BlockSpec(memory_space=pl.ANY)] * len(extra),
        out_specs=[at(model), at(cols)],
        out_shape=[
            jax.ShapeDtypeStruct((slots * rows, model), BF),
            jax.ShapeDtypeStruct((slots * rows, cols), BF),
        ],
        input_output_aliases={3: 0, 4: 1} if extra else {},
        cost_estimate=COST,
        name="project",
    )(x, gain.reshape(1, model), w, *extra)


def assemble_body(s_ref, *refs):
    out_ref = refs[-1]
    rows = refs[0].shape[0]
    for k, ref in enumerate(refs[:-1]):
        at = ((s_ref[0] ^ (k & 1)) * 2 + (s_ref[1] ^ (k >> 1))) * rows
        out_ref[pl.ds(pl.multiple_of(at, rows), rows), :] = ref[...]


def assemble(where, *pieces):
    rows, cols = pieces[0].shape
    return small_call(assemble_body, "assemble", [((4 * rows, cols), BF)], where, *pieces)[0]


def mix_body(parts, steps, x_ref, *refs):
    resid = x_ref[...].astype(F32)
    for part, weight in zip(refs[:parts], refs[parts : 2 * parts]):
        resid = resid + dg(part[...], weight[...], NN)
    refs = refs[2 * parts :]
    if steps == 0:
        refs[0][...] = resid
        return
    gain_ref, resid_ref, normed_ref = refs[:3]
    resid_ref[...] = resid
    normed = (resid * scale_of(resid) * gain_ref[...]).astype(BF)
    normed_ref[...] = normed
    for k, ref in enumerate(refs[3:]):

        @pl.when(pl.program_id(0) == k)
        def _(ref=ref):
            ref[...] = normed


def part_of(w, k, n):
    return pl.BlockSpec((n, w.shape[1]), lambda i: (k, 0))


def mix(blk, x, parts, weights, gain=None):
    rows, model = x.shape
    at = lambda c: pl.BlockSpec((blk, c), lambda i: (i, 0))
    full = lambda s: pl.BlockSpec(s, lambda i: (0, 0))
    steps = rows // blk
    shape = lambda n, t: jax.ShapeDtypeStruct((n, model), t)
    norm = gain is not None
    out = pl.pallas_call(
        functools.partial(mix_body, len(parts), steps if norm else 0),
        grid=(steps,),
        in_specs=[at(model)]
        + [at(p.shape[1]) for p in parts]
        + [part_of(w, k, n) for w, k, n in weights]
        + ([full((1, model))] if norm else []),
        out_specs=[at(model)] + ([at(model)] + [full((blk, model))] * steps if norm else []),
        out_shape=[shape(rows, F32)] + ([shape(rows, BF)] + [shape(blk, BF)] * steps if norm else []),
        cost_estimate=COST,
        name="mix",
    )(x, *parts, *[w for w, _, _ in weights], *([gain.reshape(1, model)] if norm else []))
    return (out[0], out[1], out[2:]) if norm else out[0]


def turn_body(parts, steps, weights, dy_ref, resid_ref, gain_ref, first_ref, *refs):
    rest, w_refs = refs[:parts], refs[parts : parts + weights]
    grad_ref, mixer_ref, gain_grad_ref = refs[parts + weights : parts + weights + 3]
    g_refs = refs[parts + weights + 3 :]
    grad = first_ref[...]
    for at in range(0, parts, steps):
        x = rest[at][...]
        for k in range(1, steps):
            x = jnp.where(pl.program_id(0) == k, rest[at + k][...], x)
        grad = grad + x.astype(F32)
    back, gain_grad = rms_back(resid_ref[...], gain_ref[...], grad)
    resid_grad = dy_ref[...].astype(F32) + back
    grad_ref[...] = resid_grad
    mixer = resid_grad.astype(BF)
    mixer_ref[...] = mixer
    gain_grad = jnp.sum(gain_grad.reshape(-1, 8, gain_grad.shape[-1]), axis=0)

    @pl.when(pl.program_id(0) == 0)
    def _():
        gain_grad_ref[...] = gain_grad

    @pl.when(pl.program_id(0) > 0)
    def _():
        gain_grad_ref[...] += gain_grad

    for w_ref, g_ref in zip(w_refs, g_refs):
        g_ref[...] = dg(mixer, w_ref[...], NT).astype(BF)


def turn(dy, resid, gain, first, rest, weights):
    rows, model = dy.shape
    blk = rest[0][0].shape[0]
    steps = rows // blk
    at = lambda c: pl.BlockSpec((blk, c), lambda i: (i, 0))
    full = lambda s: pl.BlockSpec(s, lambda i: (0, 0))
    rest = [x for r in rest for x in r]
    return pl.pallas_call(
        functools.partial(turn_body, len(rest), steps, len(weights)),
        grid=(steps,),
        in_specs=[at(model), at(model), full((1, model)), at(model)]
        + [full((blk, model)) for _ in rest]
        + [part_of(w, k, n) for w, k, n in weights],
        out_specs=[at(model), at(model), full((8, model))] + [at(n) for _, _, n in weights],
        out_shape=[
            jax.ShapeDtypeStruct((rows, model), F32),
            jax.ShapeDtypeStruct((rows, model), BF),
            jax.ShapeDtypeStruct((8, model), F32),
        ]
        + [jax.ShapeDtypeStruct((rows, n), BF) for _, _, n in weights],
        cost_estimate=COST,
        name="turn",
    )(dy, resid, gain.reshape(1, model), first, *rest, *[w for w, _, _ in weights])


def scale_of(rows):
    return lax.rsqrt(jnp.mean(rows * rows, axis=-1, keepdims=True) + EPSILON)


def rms_back(rows, gain, grad):
    r = scale_of(rows)
    n = rows * r
    scaled = grad * gain
    back = r * (scaled - n * jnp.mean(scaled * n, axis=-1, keepdims=True))
    return back, grad * n


def order_matrix(heads, qw):
    width = 2 * F + V
    src = lax.broadcasted_iota(jnp.int32, (heads * width, 2 * qw + heads * V), 0)
    dst = lax.broadcasted_iota(jnp.int32, (heads * width, 2 * qw + heads * V), 1)
    head, part = src // width, src % width
    target = jnp.where(
        part < F,
        head * F + part,
        jnp.where(part < 2 * F, qw + head * F + part - F, 2 * qw + head * V + part - 2 * F),
    )
    return (target == dst).astype(BF)


def per_device(
    tokens, norm1_gain, w_qkv, w_out, norm2_gain, w_gate_up, w_down, cotangent, old_mean, momentum
):
    rows, model = tokens.shape
    group = lax.axis_size("tensor")
    length = rows * group
    heads = w_qkv.shape[1] // (2 * F + V)
    hidden_units = w_down.shape[0]
    qw = -(-heads * F // LANES) * LANES
    me = lax.axis_index("tensor")
    me_arr = me.astype(jnp.int32).reshape(1)
    blk = min(256, rows)
    per = rows // blk
    sums = Sums()

    def swap(x, r):
        return lax.ppermute(x, "tensor", [(i, i ^ r) for i in range(group)])

    fast = group == 2 and sums.bits == 4 and heads * V == model // 2 and hidden_units % 32 == 0
    core, y_bit, z_bit = sums.bit(0), sums.bit(1), sums.bit(2)
    core_arr = core.reshape(1)
    others = range(1, group)
    do = Order()
    step = max(rows // 2, 128)
    cuts = range(0, rows, step)

    arrived = [swap(tokens, r) for r in others]
    order = order_matrix(heads, qw)
    w_ordered = do(lambda w: dg(w, order, NN).astype(BF), w_qkv)
    quarter = w_out.shape[0] // 4
    buffers = do(lambda x, w: project(0, group, x, norm1_gain, w, None), tokens, w_ordered)
    upstream = {(0, 0): cotangent}

    def cut_inputs(dy, w, *_):
        low = (2 * y_bit + core) * quarter
        piece = lax.dynamic_slice_in_dim(w, low, quarter, 0) if fast else w
        return piece, [dy[low : low + step] for low in cuts]

    w_piece, dy_cuts = do(cut_inputs, cotangent, w_out, *arrived)
    if fast:
        piece = swap(w_piece, 1)
    else:
        w_rest = [swap(w_out, r) for r in others]
    for r in others:
        upstream[r, 0] = swap(dy_cuts[0], r)
    for r in others:
        buffers = do(
            lambda x, *b, r=r: project(r, group, x, norm1_gain, w_ordered, b), arrived[r - 1], *buffers
        )
    normed, packed = buffers

    pairs = heads // 2
    groups = 2 if pairs % 2 == 0 else 1
    each = pairs // groups
    span = each * LANES
    attended, crossed = [], []
    for k in range(groups):
        attended.append(
            do(lambda x, k=k: attend_fwd(x, me_arr, heads, qw, blk, per, k * each, each), packed)
        )
        for r in others:
            crossed.append((k, r, swap(attended[k][1][(r - 1) * rows : r * rows], r)))
        if fast and k == 0:
            piece = do.here(piece)
            piece_y = sums.swap(piece, 1)
            piece_core = sums.swap(piece, 0)
    att_own, att_sent, attf, den, den_sum = zip(*attended)
    upstream_first = do.here(tuple(upstream[r, 0] for r in others))
    do.last = (*do.last, *upstream_first)
    if fast:
        piece_y = do.here(piece_y)
        piece_both = sums.swap(piece_y, 0)
        place_of = jnp.stack([y_bit, core])
        w_rest, _ = do(
            lambda c, x, y, p, q: (assemble(place_of, p, q, x, y), c),
            [x for k, _, x in crossed if k == 0], piece_core, piece_both, piece, piece_y,
        )
        w_rest = [w_rest]

    parts = list(att_own) + [x for _, _, x in crossed]
    blocks_of = [(0, k) for k in range(groups)] + [(r, k) for k, r, _ in crossed]
    with_blocks = lambda ws, at: [(ws[r], k, span) for r, k in at]
    for low, dy_cut in zip(cuts[1:], dy_cuts[1:]):
        for r in others:
            upstream[r, low] = swap(do.here(after(dy_cut, *parts)), r)
    resid, own2, own2_cuts = do(
        lambda x, w: mix(step, tokens, x, with_blocks(w, blocks_of), norm2_gain),
        parts, [w_out, *w_rest],
    )

    w_gate_up = jnp.swapaxes(w_gate_up, 1, 2)
    blocks = [(0, 0)] + [(r, low) for r in others for low in cuts]
    normed2, waiting = [own2], own2
    buffers = ()
    out_parts, back_parts = [], []
    for at, (r, low) in enumerate(blocks):
        if r > 0:
            x = own2_cuts[low // step]
            normed2.append(swap(x if at == 1 else after(x, waiting), r))
        kind = F32 if r == 0 else BF
        taken = [dy for (q, _), dy in upstream.items() if q > 0] if at == 1 else []
        *buffers, out_part, back_part = do(
            lambda x, dy, b, t, r=r, low=low, kind=kind: ffn(
                r * rows + low, length, x, dy, 0, w_gate_up, w_down, b or None, kind
            ),
            normed2[-1],
            upstream[r, low],
            buffers,
            taken,
        )
        if at == 0:
            waiting, first_out, first_back = out_part, out_part, back_part
        else:
            out_parts.append((out_part, r))
            back_parts.append((r, low, swap(back_part, r)))
    hidden, gate_grad, up_grad = buffers
    dy_all = [upstream[k] for k in blocks]
    back_parts = [[x for q, _, x in back_parts if q == r] for r in others]

    def finish_output(resid, first_out, *got):
        output = resid + first_out
        got = got[::-1]
        for r in others:
            count = len(cuts)
            part = got[(r - 1) * count : r * count]
            output = output + jnp.concatenate(part, axis=0).astype(F32)
        return output.astype(BF)

    def finish_norm1(p, resid_grad, *got):
        grad = dg(p[:rows], w_ordered, NT)
        for x in got:
            grad = grad + x.astype(F32)
        back, gain_grad = rms_back(tokens.astype(F32), norm1_gain, grad)
        return resid_grad + back, jnp.sum(gain_grad, axis=0)

    def halve(x, got):
        half = x.shape[0] // 2
        return add(x[:half], got[:half]), add(x[half:], got[half:])

    def qkv_halves(normed, packed_grad):
        keep, send = sums.halves(normed, 0, 1)
        return dg(keep, packed_grad, TN).astype(BF), dg(send, packed_grad, TN).astype(BF)

    def both(x, y, x_other, y_other):
        mine, theirs = sums.join(x, y, 1, 0), sums.join(x_other, y_other, 1, 0)
        cols = packed.shape[1]
        qkv = sums.join(mine[:, :cols], theirs[:, :cols], 0, 0)
        out = sums.join(mine[:, cols:], theirs[:, cols:], 0, 1)
        return dg(qkv, order, NT), out.astype(F32)

    links = [lambda x, r=r: swap(x, 1 << r) for r in range(group.bit_length() - 1)]
    links += [lambda x, b=b: sums.swap(x, b) for b in range(sums.bits)]
    by_y, by_z = jnp.stack([core, y_bit]), jnp.stack([core, z_bit])
    beside = Beside()
    now = {"bwd": 0, "packed_grad": None, "w": 0, "link": 0}
    chains = {}

    def make_ffn():
        halves = do(
            lambda lhs, n, dy, m: wgrads(lhs, n, dy, core_arr, *m),
            (gate_grad, up_grad, hidden), normed2, dy_all, [x[0] for x in back_parts],
        )
        finish = lambda *x: place(by_y, x, 2, 0, now.get("pair"))
        chains["G"] = Total(sums, do, halves[:2], (1, 2, 3), (1, 1), finish)
        finish = lambda *x: place(by_y, x, 2, 1, now.get("pair"))
        chains["U"] = Total(sums, do, halves[2:4], (1, 2, 3), (1, 1), finish)
        finish = lambda *x: place(by_z, x)
        chains["D"] = Total(sums, do, halves[4:], (2, 3, 1), (1, 1), finish)

    def make_qkv():
        halves = do(qkv_halves, normed, now["packed_grad"])
        chains["Q"] = Total(sums, do, halves, (1, 2, 3), (0, 0), both, beside)

    def step_of(name):
        def step():
            chains[name].step()
            if name in "GU" and chains[name].stage == 7:
                now["pair"] = chains[name].result

        return step

    def turn_rows():
        turned = [(r, k) for r in range(group) for k in range(groups)]
        now["resid_grad"], now["mixer"], now["gain2"], *g_all = do(
            lambda *x: turn(*x[:2], norm2_gain, x[2], x[3], with_blocks(x[4], turned)),
            cotangent, resid, first_back, back_parts, [w_out, *w_rest],
        )
        now["g_own"], now["g_sent"] = g_all[:groups], []
        for k in range(groups):
            x = [swap(g_all[r * groups + k], r) for r in others]
            now["g_sent"].append(x[0] if group == 2 else jnp.concatenate(x, axis=0))

    def make_out():
        now["wx"], send = do(
            lambda m, p, *_: wgrad_out(p, m, core_arr), now["mixer"], parts, *reversed(now["g_sent"])
        )
        now["w_flight"] = sums.swap(send, 0)

    def step_out():
        now["w"] += 1
        if now["w"] == 1:
            now["wx"], send = do(halve, now["wx"], now["w_flight"])
            now["w_flight"] = swap(send, 1)
        else:
            beside.array = do(add, now["wx"], now["w_flight"])

    def backward():
        k = now["bwd"]
        now["bwd"] += 1
        before = [] if k == 0 else [now["packed_grad"]]
        now["packed_grad"] = do(
            lambda g, s, f, d, *b: attend_bwd(
                packed, g, s, f, d, me_arr, qw, blk, per, k * each, each, *b
            ),
            now["g_own"][k], now["g_sent"][k], attf[k], den[k], *before,
        )

    def send_tokens():
        now["back1"] = []
        for r in others:
            part = do(
                lambda p, r=r: dg(p[r * rows : (r + 1) * rows], w_ordered, NT).astype(BF),
                now["packed_grad"],
            )
            now["back1"].append(swap(part, r))

    def finish_tokens():
        now["input_grad"], gain1_grad = do(
            finish_norm1, now["packed_grad"], now["resid_grad"], *now["back1"]
        )
        denom_local = sum(jnp.sum(d) for d in den_sum) * (0.5 / V)
        small = jnp.concatenate(
            [gain1_grad, jnp.sum(now["gain2"], axis=0), jnp.full((model,), denom_local / model)]
        )
        now["small"] = small.reshape(3 * model // LANES, LANES)
        now["flight"] = links[0](now["small"])

    def step_small():
        now["small"] = do(lambda x, y: x + y, now["small"], now["flight"])
        now["link"] += 1
        if now["link"] < len(links):
            now["flight"] = links[now["link"]](now["small"])

    def send_rows():
        now["got_out"] = [swap(do.here(x), k) for x, k in out_parts]

    def finish_rows():
        now["output"] = do(finish_output, resid, first_out, *reversed(now["got_out"]))

    steps = dict(
        g=make_ffn, q=make_qkv, t=turn_rows, w=make_out, W=step_out,
        A=backward, K=send_tokens, N=finish_tokens, s=step_small, O=send_rows, o=finish_rows,
        G=step_of("G"), U=step_of("U"), D=step_of("D"), Q=step_of("Q"),
    )
    for name in FAST if fast else "t" + "A" * groups + "KNOo" + "s" * len(links):
        steps[name]()
    input_grad, output, mixer_own = now["input_grad"], now["output"], now["mixer"]
    packed_grad = now["packed_grad"]
    small = now["small"].reshape(3, model)
    denom_total = jnp.sum(small[2])

    if fast:
        grad_gate_up, grad_down = now["pair"], chains["D"].result
        grad_qkv, grad_out = chains["Q"].result
    else:
        mixer_grad = jnp.concatenate([mixer_own] + [swap(mixer_own, r) for r in others], axis=0)
        att = jnp.concatenate(
            [jnp.concatenate(att_own, axis=1), jnp.concatenate(att_sent, axis=1)], axis=0
        )
        all_normed2 = jnp.concatenate(normed2, axis=0)
        all_upstream = jnp.concatenate(dy_all, axis=0)
        grad_down = dg(hidden, all_upstream, TN)
        grad_gate = dg(gate_grad, all_normed2, TN)
        grad_up = dg(up_grad, all_normed2, TN)
        grad_out = dg(att, mixer_grad, TN)
        grad_qkv = dg(dg(normed, packed_grad, TN).astype(BF), order, NT)
        grad_qkv, grad_out, grad_gate, grad_up, grad_down = lax.psum(
            (grad_qkv, grad_out, grad_gate, grad_up, grad_down), "dp"
        )
        grad_gate_up = jnp.stack([grad_gate, grad_up])
    grad_gate_up = jnp.swapaxes(grad_gate_up, 1, 2)

    rows_all = length * lax.axis_size("dp")
    per_row = heads * group * length
    mean_value = denom_total / rows_all / per_row
    new_mean = momentum * old_mean + (1.0 - momentum) * mean_value
    return (
        output,
        input_grad,
        small[0],
        grad_qkv,
        grad_out,
        small[1],
        grad_gate_up,
        grad_down,
        new_mean,
    )


def solution(mesh):
    rows = P(("dp", "tensor"), None)
    return jax.shard_map(
        per_device,
        mesh=mesh,
        in_specs=(
            rows, P(), P(None, "tensor"), P("tensor", None), P(),
            P(None, None, "tensor"), P("tensor", None), rows, P(), P(),
        ),
        out_specs=(
            rows, rows, P(), P(None, "tensor"), P("tensor", None), P(),
            P(None, None, "tensor"), P("tensor", None), P(),
        ),
        check_vma=False,
    )
```

```python
import functools

import jax
import jax.numpy as jnp
from jax import lax
from jax.experimental import pallas as pl
from jax.experimental.pallas import tpu as pltpu
from jax.sharding import PartitionSpec as P

F = 16
V = 64
EPSILON = 1e-05
F32 = jnp.float32
BF = jnp.bfloat16
NT = (((1,), (1,)), ((), ()))
NN = (((1,), (0,)), ((), ()))
TN = (((0,), (0,)), ((), ()))
LANES = 128
COST = pl.CostEstimate(flops=5 * 10**10, bytes_accessed=10**8, transcendentals=0)
SMALL = COST
FAST = (
    "gtGUDwGAUDWGAKqUDWGQUN"
    "ODGQUDGsoQsQGsUQDsUDQsQ"
)


def after(x, *others):
    return lax.optimization_barrier((x, *others))[0]


def dg(a, b, dims):
    return lax.dot_general(a, b, dims, preferred_element_type=F32)


def attend_fwd_body(blk, per, base, me_ref, q_ref, k_ref, v_ref, own_ref, sent_ref, attf_ref, den_ref, sum_ref, vals, att_s):
    length = q_ref.shape[0]
    n = length // blk
    pair = pl.program_id(0)
    flip = me_ref[0] * per

    def at(b):
        return pl.ds(pl.multiple_of((b ^ flip) * blk, blk), blk)

    vals[:, :LANES] = v_ref[...]
    eights = jnp.zeros((8, LANES), F32)

    @pl.when(pair == 0)
    def _():
        vals[:, LANES:] = jnp.ones((length, LANES), BF)

    lane = lax.broadcasted_iota(jnp.int32, (blk, LANES), 1)
    row = lax.broadcasted_iota(jnp.int32, (blk, blk), 0)
    col = lax.broadcasted_iota(jnp.int32, (blk, blk), 1)
    for i in range(n):
        query = q_ref[at(i), :]
        sums = []
        for side in range(2):
            mine = jnp.where(lane // F == 2 * (base + pair) + side, query * 0.25, 0).astype(BF)
            total = None
            for j in range(i + 1):
                t = 1.0 + dg(mine, k_ref[at(j), :], NT)
                a = t * t + 1.0
                if j == i:
                    a = jnp.where(row >= col, a, 0.0)
                part = dg(a.astype(BF), vals[at(j), :], NN)
                total = part if total is None else total + part
            sums.append(total)
        numer = jnp.where(lane < V, sums[0][:, :LANES], sums[1][:, :LANES])
        denom = jnp.where(lane < V, sums[0][:, LANES:], sums[1][:, LANES:])
        att = numer / denom
        att_s[at(i), :] = att.astype(BF)
        attf_ref[at(i), :] = att
        den_ref[at(i), :] = denom
        eights = eights + jnp.sum(denom.reshape(-1, 8, LANES), axis=0)
    sum_ref[...] = eights
    rows = own_ref.shape[0]
    own_ref[...] = att_s[:rows, :]
    sent_ref[...] = att_s[rows:, :]


def attend_fwd(packed, me, heads, qw, blk, per, base, pairs):
    length = packed.shape[0]
    rows = blk * per
    skip = 2 * qw // LANES + base
    spec = lambda index, n=length: pl.BlockSpec((n, LANES), index)
    column = lambda p, m: (0, p)
    width = LANES * pairs
    return pl.pallas_call(
        functools.partial(attend_fwd_body, blk, per, base),
        grid_spec=pltpu.PrefetchScalarGridSpec(
            num_scalar_prefetch=1,
            grid=(pairs,),
            in_specs=[
                spec(lambda p, m: (0, 0)),
                spec(lambda p, m: (0, 1)),
                spec(lambda p, m: (0, skip + p)),
            ],
            out_specs=[
                spec(column, rows),
                spec(column, length - rows),
                spec(column),
                spec(column),
                spec(column, 8),
            ],
            scratch_shapes=[pltpu.VMEM((length, 2 * LANES), BF), pltpu.VMEM((length, LANES), BF)],
        ),
        out_shape=[
            jax.ShapeDtypeStruct((rows, width), BF),
            jax.ShapeDtypeStruct((length - rows, width), BF),
            jax.ShapeDtypeStruct((length, width), F32),
            jax.ShapeDtypeStruct((length, width), F32),
            jax.ShapeDtypeStruct((8, width), F32),
        ],
        cost_estimate=COST,
        name="attend_fwd",
    )(me, packed, packed, packed)


def attend_bwd_body(blk, per, qw, base, me_ref, q_ref, k_ref, v_ref, g_own, g_sent, attf_ref, den_ref, *refs):
    out_ref, dq, q_t, g_t, dk_t, g_ref = refs[-6:]
    length = q_ref.shape[0]
    n = length // blk
    step = pl.program_id(0)
    pair = base + step
    flip = me_ref[0] * per

    def at(b):
        return pl.ds(pl.multiple_of((b ^ flip) * blk, blk), blk)

    lane = lax.broadcasted_iota(jnp.int32, (blk, LANES), 1)
    row = lax.broadcasted_iota(jnp.int32, (blk, blk), 0)
    col = lax.broadcasted_iota(jnp.int32, (blk, blk), 1)
    halves = (lane < V, lane >= V)

    @pl.when(step == 0)
    def _():
        q_t[...] = q_ref[...].T
        if base == 0:
            dq[...] = jnp.zeros_like(dq)
            dk_t[...] = jnp.zeros_like(dk_t)
        else:
            before = refs[0]
            dq[...] = before[:, :qw].astype(F32)
            dk_t[...] = before[:, qw : 2 * qw].astype(F32).T
            done = 2 * qw + LANES * base
            out_ref[:, 2 * qw : done] = before[:, 2 * qw : done]

    rows = g_own.shape[0]
    g_ref[:rows, :] = g_own[...]
    g_ref[rows:, :] = g_sent[...]
    scale = []
    for i in range(n):
        g = g_ref[at(i), :].astype(F32)
        inv = 1.0 / den_ref[at(i), :]
        ga = g * attf_ref[at(i), :]
        g_t[:, i * blk : (i + 1) * blk] = (g * inv).astype(BF).T
        for side in range(2):
            c = jnp.sum(jnp.where(halves[side], ga, 0.0), axis=1, keepdims=True)
            scale.append((c, 0.5 * inv[:, V * side : V * side + 1]))
    for j in range(n):
        key = k_ref[at(j), :]
        value = v_ref[at(j), :]
        dv = [None, None]
        dk = [None, None]
        for i in range(j, n):
            query = q_ref[at(i), :]
            g = g_ref[at(i), :]
            dq_part = None
            for side in range(2):
                head = 2 * pair + side
                q_mine = jnp.where(lane // F == head, query * 0.25, 0).astype(BF)
                g_mine = jnp.where(halves[side], g, 0).astype(BF)
                k_mine = jnp.where(lane // F == head, key, 0).astype(BF)
                t = 1.0 + dg(q_mine, key, NT)
                a = t * t + 1.0
                c, inv = scale[2 * i + side]
                ds = (dg(g_mine, value, NT) - c) * inv * t
                if i == j:
                    a = jnp.where(row >= col, a, 0.0)
                    ds = jnp.where(row >= col, ds, 0.0)
                a = a.astype(BF)
                ds = ds.astype(BF)
                x = dg(g_t[V * side : V * side + V, i * blk : (i + 1) * blk], a, NN)
                dv[side] = x if dv[side] is None else dv[side] + x
                x = dg(q_t[pl.ds(pl.multiple_of(F * head, F), F), at(i)], ds, NN)
                dk[side] = x if dk[side] is None else dk[side] + x
                x = dg(ds, k_mine, NN)
                dq_part = x if dq_part is None else dq_part + x
            dq[at(i), :] += dq_part
        lanes = pl.ds(pl.multiple_of(2 * qw + LANES * pair, LANES), LANES)
        out_ref[at(j), lanes] = jnp.concatenate(dv, axis=0).T.astype(BF)
        rows_t = pl.ds(pl.multiple_of(2 * F * pair, 2 * F), 2 * F)
        dk_t[rows_t, at(j)] = jnp.concatenate(dk, axis=0)

    @pl.when(step == pl.num_programs(0) - 1)
    def _():
        out_ref[:, :qw] = dq[...].astype(BF)
        out_ref[:, qw : 2 * qw] = dk_t[...].T.astype(BF)


def attend_bwd(packed, g_own, g_sent, attf, den, me, qw, blk, per, base, pairs, before=None):
    length, width = packed.shape
    skip = 2 * qw // LANES + base
    spec = lambda index, n=length: pl.BlockSpec((n, LANES), index)
    whole = pl.BlockSpec((length, width), lambda p, m: (0, 0))
    extra = [] if before is None else [before]
    return pl.pallas_call(
        functools.partial(attend_bwd_body, blk, per, qw, base),
        grid_spec=pltpu.PrefetchScalarGridSpec(
            num_scalar_prefetch=1,
            grid=(pairs,),
            in_specs=[
                spec(lambda p, m: (0, 0)),
                spec(lambda p, m: (0, 1)),
                spec(lambda p, m: (0, skip + p)),
                spec(lambda p, m: (0, p), g_own.shape[0]),
                spec(lambda p, m: (0, p), g_sent.shape[0]),
                spec(lambda p, m: (0, p)),
                spec(lambda p, m: (0, p)),
            ]
            + [whole] * len(extra),
            out_specs=whole,
            scratch_shapes=[
                pltpu.VMEM((length, LANES), F32),
                pltpu.VMEM((LANES, length), BF),
                pltpu.VMEM((LANES, length), BF),
                pltpu.VMEM((LANES, length), F32),
                pltpu.VMEM((length, LANES), BF),
            ],
        ),
        out_shape=jax.ShapeDtypeStruct((length, width), BF),
        cost_estimate=COST,
        name="attend_bwd",
    )(me, packed, packed, packed, g_own, g_sent, attf, den, *extra)


def ffn_body(tiles, n_ref, dy_ref, wgu_hbm, wd_hbm, *refs):
    hid_ref, gg_ref, ug_ref, out_ref, ng_ref, wgu_ref, wd_ref, sems = refs[-8:]
    copies = []
    for k, (low, high) in enumerate(tiles):
        part = pl.ds(low, high - low)
        copies.append(
            [
                pltpu.make_async_copy(wgu_hbm.at[0, part], wgu_ref.at[0, part], sems.at[k, 0]),
                pltpu.make_async_copy(wgu_hbm.at[1, part], wgu_ref.at[1, part], sems.at[k, 1]),
                pltpu.make_async_copy(wd_hbm.at[part], wd_ref.at[part], sems.at[k, 2]),
            ]
        )
        for copy in copies[-1]:
            copy.start()
    rows = n_ref[...]
    dy = dy_ref[...]
    out = None
    back = None
    for k, (low, high) in enumerate(tiles):
        for copy in copies[k]:
            copy.wait()
        w_gate = wgu_ref[0, low:high, :]
        w_up = wgu_ref[1, low:high, :]
        w_down = wd_ref[low:high, :]
        gate = dg(rows, w_gate, NT)
        upward = dg(rows, w_up, NT)
        hidden_grad = dg(dy, w_down, NT).astype(BF).astype(F32)
        sigma = 1.0 / (1.0 + jnp.exp(-gate))
        swish = gate * sigma
        hidden = (swish * upward).astype(BF)
        gate_grad = (hidden_grad * upward * sigma * (1.0 + gate * (1.0 - sigma))).astype(BF)
        up_grad = (hidden_grad * swish).astype(BF)
        hid_ref[:, low:high] = hidden
        gg_ref[:, low:high] = gate_grad
        ug_ref[:, low:high] = up_grad
        x = dg(hidden, w_down, NN)
        out = x if out is None else out + x
        x = dg(gate_grad, w_gate, NN) + dg(up_grad, w_up, NN)
        back = x if back is None else back + x
    out_ref[...] = out.astype(out_ref.dtype)
    ng_ref[...] = back.astype(ng_ref.dtype)


def ffn(start, total, n_rows, dy_rows, dy_start, w_gate_up, w_down, buffers, kind):
    model = w_down.shape[1]
    width = w_down.shape[0]
    rows = n_rows.shape[0]
    tiles = [(low, min(low + 512, width)) for low in range(0, width, 512)]
    whole = pl.BlockSpec((rows, model), lambda i: (0, 0))
    buffer_spec = pl.BlockSpec((rows, width), lambda i: (start // rows, 0))
    anywhere = pl.BlockSpec(memory_space=pl.ANY)
    extra = [] if buffers is None else list(buffers)
    return pl.pallas_call(
        functools.partial(ffn_body, tiles),
        grid=(1,),
        in_specs=[whole, pl.BlockSpec((rows, model), lambda i: (dy_start // rows, 0)), anywhere, anywhere]
        + [anywhere] * len(extra),
        out_specs=[buffer_spec] * 3 + [whole] * 2,
        out_shape=[jax.ShapeDtypeStruct((total, width), BF)] * 3
        + [jax.ShapeDtypeStruct((rows, model), kind)] * 2,
        scratch_shapes=[
            pltpu.VMEM(w_gate_up.shape, BF),
            pltpu.VMEM(w_down.shape, BF),
            pltpu.SemaphoreType.DMA((len(tiles), 3)),
        ],
        input_output_aliases={} if buffers is None else {4: 0, 5: 1, 6: 2},
        cost_estimate=COST,
        name="ffn",
    )(n_rows, dy_rows, w_gate_up, w_down, *extra)


def wgrads_body(n_count, y_count, core_ref, *refs):
    lhs_refs, refs = refs[:3], refs[3:]
    n_refs, y_refs, refs = refs[:n_count], refs[n_count : n_count + y_count], refs[n_count + y_count :]
    outs, (n_all, y_all) = refs[-8:-2], refs[-2:]
    plane = pl.program_id(0)
    first = core_ref[0] == 0
    for start, parts, whole in ((0, n_refs, n_all), (2, y_refs, y_all)):

        @pl.when((plane == start) & (pl.program_id(1) == 0))
        def _(parts=parts, whole=whole):
            at = 0
            for ref in parts:
                whole[at : at + ref.shape[0], :] = ref[...]
                at += ref.shape[0]

    for k, (lhs, rhs) in enumerate(zip(lhs_refs, (n_all, n_all, y_all))):

        @pl.when(plane == k)
        def _(k=k, lhs=lhs, rhs=rhs):
            x = dg(lhs[...], rhs[...], TN).astype(BF)
            half = x.shape[1] // 2
            outs[2 * k][...] = jnp.where(first, x[:, :half], x[:, half:])
            outs[2 * k + 1][...] = jnp.where(first, x[:, half:], x[:, :half])


def wgrads(lhs, normed2, upstream, core, *others, tile=512):
    rows, width = lhs[0].shape
    cols = normed2[0].shape[1]
    tile = min(tile, width)
    last = -(-width // tile) - 1

    def walk(k, p, i):
        return jnp.where(p == k, i, jnp.where(p < k, 0, last))

    out = lambda k: pl.BlockSpec((tile, cols // 2), lambda p, i, s: (walk(k, p, i), 0))
    return pl.pallas_call(
        functools.partial(wgrads_body, len(normed2), len(upstream)),
        grid_spec=pltpu.PrefetchScalarGridSpec(
            num_scalar_prefetch=1,
            grid=(3, last + 1),
            in_specs=[
                pl.BlockSpec((rows, tile), lambda p, i, s, k=k: (0, walk(k, p, i))) for k in range(3)
            ]
            + [pl.BlockSpec(r.shape, lambda p, i, s: (0, 0)) for r in (*normed2, *upstream)]
            + [pl.BlockSpec(memory_space=pl.ANY) for _ in others],
            out_specs=[out(k // 2) for k in range(6)],
            scratch_shapes=[pltpu.VMEM((rows, cols), BF)] * 2,
        ),
        out_shape=[jax.ShapeDtypeStruct((width, cols // 2), BF)] * 6,
        cost_estimate=COST,
        name="wgrads",
    )(core, *lhs, *normed2, *upstream, *others)


def wgrad_out_body(count, core_ref, right_ref, *refs):
    keep_ref, send_ref = refs[count:]
    right = right_ref[...]
    first = core_ref[0] == 0
    at = 0
    for ref in refs[:count]:
        x = dg(ref[...], right, TN).astype(BF)
        rows, half = x.shape[0], x.shape[1] // 2
        keep_ref[at : at + rows, :] = jnp.where(first, x[:, :half], x[:, half:])
        send_ref[at : at + rows, :] = jnp.where(first, x[:, half:], x[:, :half])
        at += rows


def wgrad_out(lefts, right, core):
    rows, cols = sum(x.shape[1] for x in lefts), right.shape[1]
    vmem = pl.BlockSpec(memory_space=pltpu.VMEM)
    return pl.pallas_call(
        functools.partial(wgrad_out_body, len(lefts)),
        in_specs=[pl.BlockSpec(memory_space=pltpu.SMEM)] + [vmem] * (1 + len(lefts)),
        out_specs=[vmem] * 2,
        out_shape=[jax.ShapeDtypeStruct((rows, cols // 2), BF)] * 2,
        cost_estimate=COST,
        name="wgrad_out",
    )(core, right, *lefts)


def small_call(body, name, outs, scalar, *arrays):
    vmem = pl.BlockSpec(memory_space=pltpu.VMEM)
    return pl.pallas_call(
        body,
        in_specs=[pl.BlockSpec(memory_space=pltpu.SMEM)] + [vmem] * len(arrays),
        out_specs=[vmem] * len(outs),
        out_shape=[jax.ShapeDtypeStruct(s, t) for s, t in outs],
        cost_estimate=SMALL,
        name=name,
    )(scalar, *arrays)


def add(x, y):
    return (x.astype(F32) + y.astype(F32)).astype(BF)


class Sums:
    def __init__(self):
        self.count = lax.axis_size("dp")
        self.bits = self.count.bit_length() - 1
        self.index = lax.axis_index("dp").astype(jnp.int32)

    def bit(self, b):
        return (self.index >> b) & 1

    def swap(self, x, b):
        return lax.ppermute(x, "dp", [(i, i ^ (1 << b)) for i in range(self.count)])

    def halves(self, x, b, axis):
        half = x.shape[axis] // 2
        low = self.bit(b) * half
        keep = lax.dynamic_slice_in_dim(x, low, half, axis)
        return keep, lax.dynamic_slice_in_dim(x, half - low, half, axis)

    def join(self, mine, got, b, axis):
        low = self.bit(b) == 0
        parts = [jnp.where(low, mine, got), jnp.where(low, got, mine)]
        return jnp.concatenate(parts, axis=axis)


class Order:
    def __init__(self):
        self.last = ()

    def __call__(self, function, *args):
        args, _ = lax.optimization_barrier((args, self.last))
        out = function(*args)
        self.last = tuple(jax.tree.leaves(out))
        return out

    def here(self, x):
        return after(x, *self.last)


class Total:
    def __init__(self, sums, do, halves, bits, axes, finish, also=None):
        self.sums, self.do, self.bits, self.axes = sums, do, bits, axes
        self.finish, self.also = finish, also
        self.x, send = halves
        self.flight = sums.swap(send, 0)
        self.stage = 0

    def step(self):
        sums, (b0, b1, b2), (a0, a1) = self.sums, self.bits, self.axes
        stage = self.stage
        self.stage += 1
        if stage < 2:
            b, axis = ((b0, a0), (b1, a1))[stage]

            def scatter(x, got, *more):
                if more:
                    x = self.also(add(x, got), *more)
                    return sums.halves(x, b, axis)
                x, got = sums.halves(x, b, axis), sums.halves(got, b, axis)
                return add(x[0], got[0]), add(x[1], got[1])

            more = self.also.more() if self.also and stage == 0 else ()
            self.x, send = self.do(scatter, self.x, self.flight, *more)
            self.flight = sums.swap(send, b)
        elif stage < 4:
            self.x = self.do(add, self.x, self.flight)
            self.flight = sums.swap(self.x, b2 if stage == 2 else b1)
        elif stage == 4:
            self.x = self.do(lambda x, got: sums.join(x, got, b1, a1), self.x, self.flight)
            self.flight = sums.swap(self.x, b0)
            self.other = sums.swap(self.x, 0)
        elif stage == 5:
            self.y = self.do.here(self.flight)
            self.do.last = (*self.do.last, self.y)
            self.flight = sums.swap(self.y, 0)
        else:
            self.result = self.do(
                lambda got, other, x, y: self.finish(x, y, other, got),
                self.flight, self.other, self.x, self.y,
            )
            return []
        return [self]


class Beside:
    def __init__(self):
        self.array = None

    def more(self):
        return (self.array,)

    def __call__(self, x, y):
        return jnp.concatenate([x, y], axis=1)


def place_body(plane, count, s_ref, *refs):
    parts, out_ref, wide, sems = refs[:count], refs[-3], refs[-2], refs[-1]
    out = out_ref if plane is None else out_ref.at[plane]
    quarter = wide.shape[2]
    copies = []
    for k, part in enumerate(parts):
        wide[k] = part[...].astype(F32)
        at = ((k >> 1) ^ s_ref[0]) * 2 + ((k & 1) ^ s_ref[1])
        columns = pl.ds(pl.multiple_of(at * quarter, quarter), quarter)
        copies.append(pltpu.make_async_copy(wide.at[k], out.at[:, columns], sems.at[k]))
        copies[-1].start()
    for copy in copies:
        copy.wait()


def place(where, parts, planes=None, plane=None, before=None):
    rows, quarter = parts[0].shape
    shape = (rows, 4 * quarter) if planes is None else (planes, rows, 4 * quarter)
    extra = [] if before is None else [before]
    anywhere = pl.BlockSpec(memory_space=pl.ANY)
    return pl.pallas_call(
        functools.partial(place_body, plane, len(parts)),
        in_specs=[pl.BlockSpec(memory_space=pltpu.SMEM)]
        + [pl.BlockSpec(memory_space=pltpu.VMEM)] * 4
        + [anywhere] * len(extra),
        out_specs=anywhere,
        out_shape=jax.ShapeDtypeStruct(shape, F32),
        scratch_shapes=[pltpu.VMEM((4, rows, quarter), F32), pltpu.SemaphoreType.DMA((4,))],
        input_output_aliases={5: 0} if extra else {},
        cost_estimate=COST,
        name="place",
    )(where, *parts, *extra)


def project_body(x_ref, gain_ref, w_ref, *refs):
    normed_ref, packed_ref = refs[-2:]
    x = x_ref[...].astype(F32)
    normed = (x * scale_of(x) * gain_ref[...]).astype(BF)
    normed_ref[...] = normed
    packed_ref[...] = dg(normed, w_ref[...], NN).astype(BF)


def project(slot, slots, x, gain, w, buffers):
    rows, model = x.shape
    cols = w.shape[1]
    blk = min(256, rows)
    steps = rows // blk
    extra = [] if buffers is None else list(buffers)
    at = lambda c: pl.BlockSpec((blk, c), lambda i: (slot * steps + i, 0))
    full = lambda s: pl.BlockSpec(s, lambda i: (0, 0))
    return pl.pallas_call(
        project_body,
        grid=(steps,),
        in_specs=[pl.BlockSpec((blk, model), lambda i: (i, 0)), full((1, model)), full(w.shape)]
        + [pl.BlockSpec(memory_space=pl.ANY)] * len(extra),
        out_specs=[at(model), at(cols)],
        out_shape=[
            jax.ShapeDtypeStruct((slots * rows, model), BF),
            jax.ShapeDtypeStruct((slots * rows, cols), BF),
        ],
        input_output_aliases={3: 0, 4: 1} if extra else {},
        cost_estimate=COST,
        name="project",
    )(x, gain.reshape(1, model), w, *extra)


def assemble_body(s_ref, *refs):
    out_ref = refs[-1]
    rows = refs[0].shape[0]
    for k, ref in enumerate(refs[:-1]):
        at = ((s_ref[0] ^ (k & 1)) * 2 + (s_ref[1] ^ (k >> 1))) * rows
        out_ref[pl.ds(pl.multiple_of(at, rows), rows), :] = ref[...]


def assemble(where, *pieces):
    rows, cols = pieces[0].shape
    return small_call(assemble_body, "assemble", [((4 * rows, cols), BF)], where, *pieces)[0]


def mix_body(parts, steps, x_ref, *refs):
    resid = x_ref[...].astype(F32)
    for part, weight in zip(refs[:parts], refs[parts : 2 * parts]):
        resid = resid + dg(part[...], weight[...], NN)
    refs = refs[2 * parts :]
    if steps == 0:
        refs[0][...] = resid
        return
    gain_ref, resid_ref, normed_ref = refs[:3]
    resid_ref[...] = resid
    normed = (resid * scale_of(resid) * gain_ref[...]).astype(BF)
    normed_ref[...] = normed
    for k, ref in enumerate(refs[3:]):

        @pl.when(pl.program_id(0) == k)
        def _(ref=ref):
            ref[...] = normed


def part_of(w, k, n):
    return pl.BlockSpec((n, w.shape[1]), lambda i: (k, 0))


def mix(blk, x, parts, weights, gain=None):
    rows, model = x.shape
    at = lambda c: pl.BlockSpec((blk, c), lambda i: (i, 0))
    full = lambda s: pl.BlockSpec(s, lambda i: (0, 0))
    steps = rows // blk
    shape = lambda n, t: jax.ShapeDtypeStruct((n, model), t)
    norm = gain is not None
    out = pl.pallas_call(
        functools.partial(mix_body, len(parts), steps if norm else 0),
        grid=(steps,),
        in_specs=[at(model)]
        + [at(p.shape[1]) for p in parts]
        + [part_of(w, k, n) for w, k, n in weights]
        + ([full((1, model))] if norm else []),
        out_specs=[at(model)] + ([at(model)] + [full((blk, model))] * steps if norm else []),
        out_shape=[shape(rows, F32)] + ([shape(rows, BF)] + [shape(blk, BF)] * steps if norm else []),
        cost_estimate=COST,
        name="mix",
    )(x, *parts, *[w for w, _, _ in weights], *([gain.reshape(1, model)] if norm else []))
    return (out[0], out[1], out[2:]) if norm else out[0]


def turn_body(parts, steps, weights, dy_ref, resid_ref, gain_ref, first_ref, *refs):
    rest, w_refs = refs[:parts], refs[parts : parts + weights]
    grad_ref, mixer_ref, gain_grad_ref = refs[parts + weights : parts + weights + 3]
    g_refs = refs[parts + weights + 3 :]
    grad = first_ref[...]
    for at in range(0, parts, steps):
        x = rest[at][...]
        for k in range(1, steps):
            x = jnp.where(pl.program_id(0) == k, rest[at + k][...], x)
        grad = grad + x.astype(F32)
    back, gain_grad = rms_back(resid_ref[...], gain_ref[...], grad)
    resid_grad = dy_ref[...].astype(F32) + back
    grad_ref[...] = resid_grad
    mixer = resid_grad.astype(BF)
    mixer_ref[...] = mixer
    gain_grad = jnp.sum(gain_grad.reshape(-1, 8, gain_grad.shape[-1]), axis=0)

    @pl.when(pl.program_id(0) == 0)
    def _():
        gain_grad_ref[...] = gain_grad

    @pl.when(pl.program_id(0) > 0)
    def _():
        gain_grad_ref[...] += gain_grad

    for w_ref, g_ref in zip(w_refs, g_refs):
        g_ref[...] = dg(mixer, w_ref[...], NT).astype(BF)


def turn(dy, resid, gain, first, rest, weights):
    rows, model = dy.shape
    blk = rest[0][0].shape[0]
    steps = rows // blk
    at = lambda c: pl.BlockSpec((blk, c), lambda i: (i, 0))
    full = lambda s: pl.BlockSpec(s, lambda i: (0, 0))
    rest = [x for r in rest for x in r]
    return pl.pallas_call(
        functools.partial(turn_body, len(rest), steps, len(weights)),
        grid=(steps,),
        in_specs=[at(model), at(model), full((1, model)), at(model)]
        + [full((blk, model)) for _ in rest]
        + [part_of(w, k, n) for w, k, n in weights],
        out_specs=[at(model), at(model), full((8, model))] + [at(n) for _, _, n in weights],
        out_shape=[
            jax.ShapeDtypeStruct((rows, model), F32),
            jax.ShapeDtypeStruct((rows, model), BF),
            jax.ShapeDtypeStruct((8, model), F32),
        ]
        + [jax.ShapeDtypeStruct((rows, n), BF) for _, _, n in weights],
        cost_estimate=COST,
        name="turn",
    )(dy, resid, gain.reshape(1, model), first, *rest, *[w for w, _, _ in weights])


def scale_of(rows):
    return lax.rsqrt(jnp.mean(rows * rows, axis=-1, keepdims=True) + EPSILON)


def rms_back(rows, gain, grad):
    r = scale_of(rows)
    n = rows * r
    scaled = grad * gain
    back = r * (scaled - n * jnp.mean(scaled * n, axis=-1, keepdims=True))
    return back, grad * n


def order_matrix(heads, qw):
    width = 2 * F + V
    src = lax.broadcasted_iota(jnp.int32, (heads * width, 2 * qw + heads * V), 0)
    dst = lax.broadcasted_iota(jnp.int32, (heads * width, 2 * qw + heads * V), 1)
    head, part = src // width, src % width
    target = jnp.where(
        part < F,
        head * F + part,
        jnp.where(part < 2 * F, qw + head * F + part - F, 2 * qw + head * V + part - 2 * F),
    )
    return (target == dst).astype(BF)


def per_device(
    tokens, norm1_gain, w_qkv, w_out, norm2_gain, w_gate_up, w_down, cotangent, old_mean, momentum
):
    rows, model = tokens.shape
    group = lax.axis_size("tensor")
    length = rows * group
    heads = w_qkv.shape[1] // (2 * F + V)
    hidden_units = w_down.shape[0]
    qw = -(-heads * F // LANES) * LANES
    me = lax.axis_index("tensor")
    me_arr = me.astype(jnp.int32).reshape(1)
    blk = min(256, rows)
    per = rows // blk
    sums = Sums()

    def swap(x, r):
        return lax.ppermute(x, "tensor", [(i, i ^ r) for i in range(group)])

    fast = group == 2 and sums.bits == 4 and heads * V == model // 2 and hidden_units % 32 == 0
    core, y_bit, z_bit = sums.bit(0), sums.bit(1), sums.bit(2)
    core_arr = core.reshape(1)
    others = range(1, group)
    do = Order()
    step = max(rows // 2, 128)
    cuts = range(0, rows, step)

    arrived = [swap(tokens, r) for r in others]
    order = order_matrix(heads, qw)
    w_ordered = do(lambda w: dg(w, order, NN).astype(BF), w_qkv)
    quarter = w_out.shape[0] // 4
    buffers = do(lambda x, w: project(0, group, x, norm1_gain, w, None), tokens, w_ordered)
    upstream = {(0, 0): cotangent}

    def cut_inputs(dy, w, *_):
        low = (2 * y_bit + core) * quarter
        piece = lax.dynamic_slice_in_dim(w, low, quarter, 0) if fast else w
        return piece, [dy[low : low + step] for low in cuts]

    w_piece, dy_cuts = do(cut_inputs, cotangent, w_out, *arrived)
    if fast:
        piece = swap(w_piece, 1)
    else:
        w_rest = [swap(w_out, r) for r in others]
    for r in others:
        upstream[r, 0] = swap(dy_cuts[0], r)
    for r in others:
        buffers = do(
            lambda x, *b, r=r: project(r, group, x, norm1_gain, w_ordered, b), arrived[r - 1], *buffers
        )
    normed, packed = buffers

    pairs = heads // 2
    groups = 2 if pairs % 2 == 0 else 1
    each = pairs // groups
    span = each * LANES
    attended, crossed = [], []
    for k in range(groups):
        attended.append(
            do(lambda x, k=k: attend_fwd(x, me_arr, heads, qw, blk, per, k * each, each), packed)
        )
        for r in others:
            crossed.append((k, r, swap(attended[k][1][(r - 1) * rows : r * rows], r)))
        if fast and k == 0:
            piece = do.here(piece)
            piece_y = sums.swap(piece, 1)
            piece_core = sums.swap(piece, 0)
    att_own, att_sent, attf, den, den_sum = zip(*attended)
    upstream_first = do.here(tuple(upstream[r, 0] for r in others))
    do.last = (*do.last, *upstream_first)
    if fast:
        piece_y = do.here(piece_y)
        piece_both = sums.swap(piece_y, 0)
        place_of = jnp.stack([y_bit, core])
        w_rest, _ = do(
            lambda c, x, y, p, q: (assemble(place_of, p, q, x, y), c),
            [x for k, _, x in crossed if k == 0], piece_core, piece_both, piece, piece_y,
        )
        w_rest = [w_rest]

    parts = list(att_own) + [x for _, _, x in crossed]
    blocks_of = [(0, k) for k in range(groups)] + [(r, k) for k, r, _ in crossed]
    with_blocks = lambda ws, at: [(ws[r], k, span) for r, k in at]
    for low, dy_cut in zip(cuts[1:], dy_cuts[1:]):
        for r in others:
            upstream[r, low] = swap(do.here(after(dy_cut, *parts)), r)
    resid, own2, own2_cuts = do(
        lambda x, w: mix(step, tokens, x, with_blocks(w, blocks_of), norm2_gain),
        parts, [w_out, *w_rest],
    )

    w_gate_up = jnp.swapaxes(w_gate_up, 1, 2)
    blocks = [(0, 0)] + [(r, low) for r in others for low in cuts]
    normed2, waiting = [own2], own2
    buffers = ()
    out_parts, back_parts = [], []
    for at, (r, low) in enumerate(blocks):
        if r > 0:
            x = own2_cuts[low // step]
            normed2.append(swap(x if at == 1 else after(x, waiting), r))
        kind = F32 if r == 0 else BF
        taken = [dy for (q, _), dy in upstream.items() if q > 0] if at == 1 else []
        *buffers, out_part, back_part = do(
            lambda x, dy, b, t, r=r, low=low, kind=kind: ffn(
                r * rows + low, length, x, dy, 0, w_gate_up, w_down, b or None, kind
            ),
            normed2[-1],
            upstream[r, low],
            buffers,
            taken,
        )
        if at == 0:
            waiting, first_out, first_back = out_part, out_part, back_part
        else:
            out_parts.append((out_part, r))
            back_parts.append((r, low, swap(back_part, r)))
    hidden, gate_grad, up_grad = buffers
    dy_all = [upstream[k] for k in blocks]
    back_parts = [[x for q, _, x in back_parts if q == r] for r in others]

    def finish_output(resid, first_out, *got):
        output = resid + first_out
        got = got[::-1]
        for r in others:
            count = len(cuts)
            part = got[(r - 1) * count : r * count]
            output = output + jnp.concatenate(part, axis=0).astype(F32)
        return output.astype(BF)

    def finish_norm1(p, resid_grad, *got):
        grad = dg(p[:rows], w_ordered, NT)
        for x in got:
            grad = grad + x.astype(F32)
        back, gain_grad = rms_back(tokens.astype(F32), norm1_gain, grad)
        return resid_grad + back, jnp.sum(gain_grad, axis=0)

    def halve(x, got):
        half = x.shape[0] // 2
        return add(x[:half], got[:half]), add(x[half:], got[half:])

    def qkv_halves(normed, packed_grad):
        keep, send = sums.halves(normed, 0, 1)
        return dg(keep, packed_grad, TN).astype(BF), dg(send, packed_grad, TN).astype(BF)

    def both(x, y, x_other, y_other):
        mine, theirs = sums.join(x, y, 1, 0), sums.join(x_other, y_other, 1, 0)
        cols = packed.shape[1]
        qkv = sums.join(mine[:, :cols], theirs[:, :cols], 0, 0)
        out = sums.join(mine[:, cols:], theirs[:, cols:], 0, 1)
        return dg(qkv, order, NT), out.astype(F32)

    links = [lambda x, r=r: swap(x, 1 << r) for r in range(group.bit_length() - 1)]
    links += [lambda x, b=b: sums.swap(x, b) for b in range(sums.bits)]
    by_y, by_z = jnp.stack([core, y_bit]), jnp.stack([core, z_bit])
    beside = Beside()
    now = {"bwd": 0, "packed_grad": None, "w": 0, "link": 0}
    chains = {}

    def make_ffn():
        halves = do(
            lambda lhs, n, dy, m: wgrads(lhs, n, dy, core_arr, *m),
            (gate_grad, up_grad, hidden), normed2, dy_all, [x[0] for x in back_parts],
        )
        finish = lambda *x: place(by_y, x, 2, 0, now.get("pair"))
        chains["G"] = Total(sums, do, halves[:2], (1, 2, 3), (1, 1), finish)
        finish = lambda *x: place(by_y, x, 2, 1, now.get("pair"))
        chains["U"] = Total(sums, do, halves[2:4], (1, 2, 3), (1, 1), finish)
        finish = lambda *x: place(by_z, x)
        chains["D"] = Total(sums, do, halves[4:], (2, 3, 1), (1, 1), finish)

    def make_qkv():
        halves = do(qkv_halves, normed, now["packed_grad"])
        chains["Q"] = Total(sums, do, halves, (1, 2, 3), (0, 0), both, beside)

    def step_of(name):
        def step():
            chains[name].step()
            if name in "GU" and chains[name].stage == 7:
                now["pair"] = chains[name].result

        return step

    def turn_rows():
        turned = [(r, k) for r in range(group) for k in range(groups)]
        now["resid_grad"], now["mixer"], now["gain2"], *g_all = do(
            lambda *x: turn(*x[:2], norm2_gain, x[2], x[3], with_blocks(x[4], turned)),
            cotangent, resid, first_back, back_parts, [w_out, *w_rest],
        )
        now["g_own"], now["g_sent"] = g_all[:groups], []
        for k in range(groups):
            x = [swap(g_all[r * groups + k], r) for r in others]
            now["g_sent"].append(x[0] if group == 2 else jnp.concatenate(x, axis=0))

    def make_out():
        now["wx"], send = do(
            lambda m, p, *_: wgrad_out(p, m, core_arr), now["mixer"], parts, *reversed(now["g_sent"])
        )
        now["w_flight"] = sums.swap(send, 0)

    def step_out():
        now["w"] += 1
        if now["w"] == 1:
            now["wx"], send = do(halve, now["wx"], now["w_flight"])
            now["w_flight"] = swap(send, 1)
        else:
            beside.array = do(add, now["wx"], now["w_flight"])

    def backward():
        k = now["bwd"]
        now["bwd"] += 1
        before = [] if k == 0 else [now["packed_grad"]]
        now["packed_grad"] = do(
            lambda g, s, f, d, *b: attend_bwd(
                packed, g, s, f, d, me_arr, qw, rows, 1, k * each, each, *b
            ),
            now["g_own"][k], now["g_sent"][k], attf[k], den[k], *before,
        )

    def send_tokens():
        now["back1"] = []
        for r in others:
            part = do(
                lambda p, r=r: dg(p[r * rows : (r + 1) * rows], w_ordered, NT).astype(BF),
                now["packed_grad"],
            )
            now["back1"].append(swap(part, r))

    def finish_tokens():
        now["input_grad"], gain1_grad = do(
            finish_norm1, now["packed_grad"], now["resid_grad"], *now["back1"]
        )
        denom_local = sum(jnp.sum(d) for d in den_sum) * (0.5 / V)
        small = jnp.concatenate(
            [gain1_grad, jnp.sum(now["gain2"], axis=0), jnp.full((model,), denom_local / model)]
        )
        now["small"] = small.reshape(3 * model // LANES, LANES)
        now["flight"] = links[0](now["small"])

    def step_small():
        now["small"] = do(lambda x, y: x + y, now["small"], now["flight"])
        now["link"] += 1
        if now["link"] < len(links):
            now["flight"] = links[now["link"]](now["small"])

    def send_rows():
        now["got_out"] = [swap(do.here(x), k) for x, k in out_parts]

    def finish_rows():
        now["output"] = do(finish_output, resid, first_out, *reversed(now["got_out"]))

    steps = dict(
        g=make_ffn, q=make_qkv, t=turn_rows, w=make_out, W=step_out,
        A=backward, K=send_tokens, N=finish_tokens, s=step_small, O=send_rows, o=finish_rows,
        G=step_of("G"), U=step_of("U"), D=step_of("D"), Q=step_of("Q"),
    )
    for name in FAST if fast else "t" + "A" * groups + "KNOo" + "s" * len(links):
        steps[name]()
    input_grad, output, mixer_own = now["input_grad"], now["output"], now["mixer"]
    packed_grad = now["packed_grad"]
    small = now["small"].reshape(3, model)
    denom_total = jnp.sum(small[2])

    if fast:
        grad_gate_up, grad_down = now["pair"], chains["D"].result
        grad_qkv, grad_out = chains["Q"].result
    else:
        mixer_grad = jnp.concatenate([mixer_own] + [swap(mixer_own, r) for r in others], axis=0)
        att = jnp.concatenate(
            [jnp.concatenate(att_own, axis=1), jnp.concatenate(att_sent, axis=1)], axis=0
        )
        all_normed2 = jnp.concatenate(normed2, axis=0)
        all_upstream = jnp.concatenate(dy_all, axis=0)
        grad_down = dg(hidden, all_upstream, TN)
        grad_gate = dg(gate_grad, all_normed2, TN)
        grad_up = dg(up_grad, all_normed2, TN)
        grad_out = dg(att, mixer_grad, TN)
        grad_qkv = dg(dg(normed, packed_grad, TN).astype(BF), order, NT)
        grad_qkv, grad_out, grad_gate, grad_up, grad_down = lax.psum(
            (grad_qkv, grad_out, grad_gate, grad_up, grad_down), "dp"
        )
        grad_gate_up = jnp.stack([grad_gate, grad_up])
    grad_gate_up = jnp.swapaxes(grad_gate_up, 1, 2)

    rows_all = length * lax.axis_size("dp")
    per_row = heads * group * length
    mean_value = denom_total / rows_all / per_row
    new_mean = momentum * old_mean + (1.0 - momentum) * mean_value
    return (
        output,
        input_grad,
        small[0],
        grad_qkv,
        grad_out,
        small[1],
        grad_gate_up,
        grad_down,
        new_mean,
    )


def solution(mesh):
    rows = P(("dp", "tensor"), None)
    return jax.shard_map(
        per_device,
        mesh=mesh,
        in_specs=(
            rows, P(), P(None, "tensor"), P("tensor", None), P(),
            P(None, None, "tensor"), P("tensor", None), rows, P(), P(),
        ),
        out_specs=(
            rows, rows, P(), P(None, "tensor"), P("tensor", None), P(),
            P(None, None, "tensor"), P("tensor", None), P(),
        ),
        check_vma=False,
    )
```

```python
import functools

import jax
import jax.numpy as jnp
from jax import lax
from jax.experimental import pallas as pl
from jax.experimental.pallas import tpu as pltpu
from jax.sharding import PartitionSpec as P

F = 16
V = 64
EPSILON = 1e-05
F32 = jnp.float32
BF = jnp.bfloat16
NT = (((1,), (1,)), ((), ()))
NN = (((1,), (0,)), ((), ()))
TN = (((0,), (0,)), ((), ()))
LANES = 128
COST = pl.CostEstimate(flops=5 * 10**10, bytes_accessed=10**8, transcendentals=0)
SMALL = COST
FAST = (
    "gtGUDwGAUDWGAKqUDWGQNO"
    "UDGQUDGsoQsQGsUQDsUDQsQ"
)


def after(x, *others):
    return lax.optimization_barrier((x, *others))[0]


def dg(a, b, dims):
    return lax.dot_general(a, b, dims, preferred_element_type=F32)


def attend_fwd_body(blk, per, base, me_ref, q_ref, k_ref, v_ref, own_ref, sent_ref, attf_ref, den_ref, sum_ref, vals, att_s):
    length = q_ref.shape[0]
    n = length // blk
    pair = pl.program_id(0)
    flip = me_ref[0] * per

    def at(b):
        return pl.ds(pl.multiple_of((b ^ flip) * blk, blk), blk)

    vals[:, :LANES] = v_ref[...]
    eights = jnp.zeros((8, LANES), F32)

    @pl.when(pair == 0)
    def _():
        vals[:, LANES:] = jnp.ones((length, LANES), BF)

    lane = lax.broadcasted_iota(jnp.int32, (blk, LANES), 1)
    row = lax.broadcasted_iota(jnp.int32, (blk, blk), 0)
    col = lax.broadcasted_iota(jnp.int32, (blk, blk), 1)
    for i in range(n):
        query = q_ref[at(i), :]
        sums = []
        for side in range(2):
            mine = jnp.where(lane // F == 2 * (base + pair) + side, query * 0.25, 0).astype(BF)
            total = None
            for j in range(i + 1):
                t = 1.0 + dg(mine, k_ref[at(j), :], NT)
                a = t * t + 1.0
                if j == i:
                    a = jnp.where(row >= col, a, 0.0)
                part = dg(a.astype(BF), vals[at(j), :], NN)
                total = part if total is None else total + part
            sums.append(total)
        numer = jnp.where(lane < V, sums[0][:, :LANES], sums[1][:, :LANES])
        denom = jnp.where(lane < V, sums[0][:, LANES:], sums[1][:, LANES:])
        att = numer / denom
        att_s[at(i), :] = att.astype(BF)
        attf_ref[at(i), :] = att
        den_ref[at(i), :] = denom
        eights = eights + jnp.sum(denom.reshape(-1, 8, LANES), axis=0)
    sum_ref[...] = eights
    rows = own_ref.shape[0]
    own_ref[...] = att_s[:rows, :]
    sent_ref[...] = att_s[rows:, :]


def attend_fwd(packed, me, heads, qw, blk, per, base, pairs):
    length = packed.shape[0]
    rows = blk * per
    skip = 2 * qw // LANES + base
    spec = lambda index, n=length: pl.BlockSpec((n, LANES), index)
    column = lambda p, m: (0, p)
    width = LANES * pairs
    return pl.pallas_call(
        functools.partial(attend_fwd_body, blk, per, base),
        grid_spec=pltpu.PrefetchScalarGridSpec(
            num_scalar_prefetch=1,
            grid=(pairs,),
            in_specs=[
                spec(lambda p, m: (0, 0)),
                spec(lambda p, m: (0, 1)),
                spec(lambda p, m: (0, skip + p)),
            ],
            out_specs=[
                spec(column, rows),
                spec(column, length - rows),
                spec(column),
                spec(column),
                spec(column, 8),
            ],
            scratch_shapes=[pltpu.VMEM((length, 2 * LANES), BF), pltpu.VMEM((length, LANES), BF)],
        ),
        out_shape=[
            jax.ShapeDtypeStruct((rows, width), BF),
            jax.ShapeDtypeStruct((length - rows, width), BF),
            jax.ShapeDtypeStruct((length, width), F32),
            jax.ShapeDtypeStruct((length, width), F32),
            jax.ShapeDtypeStruct((8, width), F32),
        ],
        cost_estimate=COST,
        name="attend_fwd",
    )(me, packed, packed, packed)


def attend_bwd_body(blk, per, qw, base, me_ref, q_ref, k_ref, v_ref, g_own, g_sent, attf_ref, den_ref, *refs):
    out_ref, dq, q_t, g_t, dk_t, g_ref = refs[-6:]
    length = q_ref.shape[0]
    n = length // blk
    step = pl.program_id(0)
    pair = base + step
    flip = me_ref[0] * per

    def at(b):
        return pl.ds(pl.multiple_of((b ^ flip) * blk, blk), blk)

    lane = lax.broadcasted_iota(jnp.int32, (blk, LANES), 1)
    row = lax.broadcasted_iota(jnp.int32, (blk, blk), 0)
    col = lax.broadcasted_iota(jnp.int32, (blk, blk), 1)
    halves = (lane < V, lane >= V)

    @pl.when(step == 0)
    def _():
        q_t[...] = q_ref[...].T
        if base == 0:
            dq[...] = jnp.zeros_like(dq)
            dk_t[...] = jnp.zeros_like(dk_t)
        else:
            before = refs[0]
            dq[...] = before[:, :qw].astype(F32)
            dk_t[...] = before[:, qw : 2 * qw].astype(F32).T
            done = 2 * qw + LANES * base
            out_ref[:, 2 * qw : done] = before[:, 2 * qw : done]

    rows = g_own.shape[0]
    g_ref[:rows, :] = g_own[...]
    g_ref[rows:, :] = g_sent[...]
    scale = []
    for i in range(n):
        g = g_ref[at(i), :].astype(F32)
        inv = 1.0 / den_ref[at(i), :]
        ga = g * attf_ref[at(i), :]
        g_t[:, i * blk : (i + 1) * blk] = (g * inv).astype(BF).T
        for side in range(2):
            c = jnp.sum(jnp.where(halves[side], ga, 0.0), axis=1, keepdims=True)
            scale.append((c, 0.5 * inv[:, V * side : V * side + 1]))
    for j in range(n):
        key = k_ref[at(j), :]
        value = v_ref[at(j), :]
        dv = [None, None]
        dk = [None, None]
        for i in range(j, n):
            query = q_ref[at(i), :]
            g = g_ref[at(i), :]
            dq_part = None
            for side in range(2):
                head = 2 * pair + side
                q_mine = jnp.where(lane // F == head, query * 0.25, 0).astype(BF)
                g_mine = jnp.where(halves[side], g, 0).astype(BF)
                k_mine = jnp.where(lane // F == head, key, 0).astype(BF)
                t = 1.0 + dg(q_mine, key, NT)
                a = t * t + 1.0
                c, inv = scale[2 * i + side]
                ds = (dg(g_mine, value, NT) - c) * inv * t
                if i == j:
                    a = jnp.where(row >= col, a, 0.0)
                    ds = jnp.where(row >= col, ds, 0.0)
                a = a.astype(BF)
                ds = ds.astype(BF)
                x = dg(g_t[V * side : V * side + V, i * blk : (i + 1) * blk], a, NN)
                dv[side] = x if dv[side] is None else dv[side] + x
                x = dg(q_t[pl.ds(pl.multiple_of(F * head, F), F), at(i)], ds, NN)
                dk[side] = x if dk[side] is None else dk[side] + x
                x = dg(ds, k_mine, NN)
                dq_part = x if dq_part is None else dq_part + x
            dq[at(i), :] += dq_part
        lanes = pl.ds(pl.multiple_of(2 * qw + LANES * pair, LANES), LANES)
        out_ref[at(j), lanes] = jnp.concatenate(dv, axis=0).T.astype(BF)
        rows_t = pl.ds(pl.multiple_of(2 * F * pair, 2 * F), 2 * F)
        dk_t[rows_t, at(j)] = jnp.concatenate(dk, axis=0)

    @pl.when(step == pl.num_programs(0) - 1)
    def _():
        out_ref[:, :qw] = dq[...].astype(BF)
        out_ref[:, qw : 2 * qw] = dk_t[...].T.astype(BF)


def attend_bwd(packed, g_own, g_sent, attf, den, me, qw, blk, per, base, pairs, before=None):
    length, width = packed.shape
    skip = 2 * qw // LANES + base
    spec = lambda index, n=length: pl.BlockSpec((n, LANES), index)
    whole = pl.BlockSpec((length, width), lambda p, m: (0, 0))
    extra = [] if before is None else [before]
    return pl.pallas_call(
        functools.partial(attend_bwd_body, blk, per, qw, base),
        grid_spec=pltpu.PrefetchScalarGridSpec(
            num_scalar_prefetch=1,
            grid=(pairs,),
            in_specs=[
                spec(lambda p, m: (0, 0)),
                spec(lambda p, m: (0, 1)),
                spec(lambda p, m: (0, skip + p)),
                spec(lambda p, m: (0, p), g_own.shape[0]),
                spec(lambda p, m: (0, p), g_sent.shape[0]),
                spec(lambda p, m: (0, p)),
                spec(lambda p, m: (0, p)),
            ]
            + [whole] * len(extra),
            out_specs=whole,
            scratch_shapes=[
                pltpu.VMEM((length, LANES), F32),
                pltpu.VMEM((LANES, length), BF),
                pltpu.VMEM((LANES, length), BF),
                pltpu.VMEM((LANES, length), F32),
                pltpu.VMEM((length, LANES), BF),
            ],
        ),
        out_shape=jax.ShapeDtypeStruct((length, width), BF),
        cost_estimate=COST,
        name="attend_bwd",
    )(me, packed, packed, packed, g_own, g_sent, attf, den, *extra)


def ffn_body(tiles, n_ref, dy_ref, wgu_hbm, wd_hbm, *refs):
    hid_ref, gg_ref, ug_ref, out_ref, ng_ref, wgu_ref, wd_ref, sems = refs[-8:]
    copies = []
    for k, (low, high) in enumerate(tiles):
        part = pl.ds(low, high - low)
        copies.append(
            [
                pltpu.make_async_copy(wgu_hbm.at[0, part], wgu_ref.at[0, part], sems.at[k, 0]),
                pltpu.make_async_copy(wgu_hbm.at[1, part], wgu_ref.at[1, part], sems.at[k, 1]),
                pltpu.make_async_copy(wd_hbm.at[part], wd_ref.at[part], sems.at[k, 2]),
            ]
        )
        for copy in copies[-1]:
            copy.start()
    rows = n_ref[...]
    dy = dy_ref[...]
    out = None
    back = None
    for k, (low, high) in enumerate(tiles):
        for copy in copies[k]:
            copy.wait()
        w_gate = wgu_ref[0, low:high, :]
        w_up = wgu_ref[1, low:high, :]
        w_down = wd_ref[low:high, :]
        gate = dg(rows, w_gate, NT)
        upward = dg(rows, w_up, NT)
        hidden_grad = dg(dy, w_down, NT).astype(BF).astype(F32)
        sigma = 1.0 / (1.0 + jnp.exp(-gate))
        swish = gate * sigma
        hidden = (swish * upward).astype(BF)
        gate_grad = (hidden_grad * upward * sigma * (1.0 + gate * (1.0 - sigma))).astype(BF)
        up_grad = (hidden_grad * swish).astype(BF)
        hid_ref[:, low:high] = hidden
        gg_ref[:, low:high] = gate_grad
        ug_ref[:, low:high] = up_grad
        x = dg(hidden, w_down, NN)
        out = x if out is None else out + x
        x = dg(gate_grad, w_gate, NN) + dg(up_grad, w_up, NN)
        back = x if back is None else back + x
    out_ref[...] = out.astype(out_ref.dtype)
    ng_ref[...] = back.astype(ng_ref.dtype)


def ffn(start, total, n_rows, dy_rows, dy_start, w_gate_up, w_down, buffers, kind):
    model = w_down.shape[1]
    width = w_down.shape[0]
    rows = n_rows.shape[0]
    tiles = [(low, min(low + 512, width)) for low in range(0, width, 512)]
    whole = pl.BlockSpec((rows, model), lambda i: (0, 0))
    buffer_spec = pl.BlockSpec((rows, width), lambda i: (start // rows, 0))
    anywhere = pl.BlockSpec(memory_space=pl.ANY)
    extra = [] if buffers is None else list(buffers)
    return pl.pallas_call(
        functools.partial(ffn_body, tiles),
        grid=(1,),
        in_specs=[whole, pl.BlockSpec((rows, model), lambda i: (dy_start // rows, 0)), anywhere, anywhere]
        + [anywhere] * len(extra),
        out_specs=[buffer_spec] * 3 + [whole] * 2,
        out_shape=[jax.ShapeDtypeStruct((total, width), BF)] * 3
        + [jax.ShapeDtypeStruct((rows, model), kind)] * 2,
        scratch_shapes=[
            pltpu.VMEM(w_gate_up.shape, BF),
            pltpu.VMEM(w_down.shape, BF),
            pltpu.SemaphoreType.DMA((len(tiles), 3)),
        ],
        input_output_aliases={} if buffers is None else {4: 0, 5: 1, 6: 2},
        cost_estimate=COST,
        name="ffn",
    )(n_rows, dy_rows, w_gate_up, w_down, *extra)


def wgrads_body(n_count, y_count, core_ref, *refs):
    lhs_refs, refs = refs[:3], refs[3:]
    n_refs, y_refs, refs = refs[:n_count], refs[n_count : n_count + y_count], refs[n_count + y_count :]
    outs, (n_all, y_all) = refs[-8:-2], refs[-2:]
    plane = pl.program_id(0)
    first = core_ref[0] == 0
    for start, parts, whole in ((0, n_refs, n_all), (2, y_refs, y_all)):

        @pl.when((plane == start) & (pl.program_id(1) == 0))
        def _(parts=parts, whole=whole):
            at = 0
            for ref in parts:
                whole[at : at + ref.shape[0], :] = ref[...]
                at += ref.shape[0]

    for k, (lhs, rhs) in enumerate(zip(lhs_refs, (n_all, n_all, y_all))):

        @pl.when(plane == k)
        def _(k=k, lhs=lhs, rhs=rhs):
            x = dg(lhs[...], rhs[...], TN).astype(BF)
            half = x.shape[1] // 2
            outs[2 * k][...] = jnp.where(first, x[:, :half], x[:, half:])
            outs[2 * k + 1][...] = jnp.where(first, x[:, half:], x[:, :half])


def wgrads(lhs, normed2, upstream, core, *others, tile=512):
    rows, width = lhs[0].shape
    cols = normed2[0].shape[1]
    tile = min(tile, width)
    last = -(-width // tile) - 1

    def walk(k, p, i):
        return jnp.where(p == k, i, jnp.where(p < k, 0, last))

    out = lambda k: pl.BlockSpec((tile, cols // 2), lambda p, i, s: (walk(k, p, i), 0))
    return pl.pallas_call(
        functools.partial(wgrads_body, len(normed2), len(upstream)),
        grid_spec=pltpu.PrefetchScalarGridSpec(
            num_scalar_prefetch=1,
            grid=(3, last + 1),
            in_specs=[
                pl.BlockSpec((rows, tile), lambda p, i, s, k=k: (0, walk(k, p, i))) for k in range(3)
            ]
            + [pl.BlockSpec(r.shape, lambda p, i, s: (0, 0)) for r in (*normed2, *upstream)]
            + [pl.BlockSpec(memory_space=pl.ANY) for _ in others],
            out_specs=[out(k // 2) for k in range(6)],
            scratch_shapes=[pltpu.VMEM((rows, cols), BF)] * 2,
        ),
        out_shape=[jax.ShapeDtypeStruct((width, cols // 2), BF)] * 6,
        cost_estimate=COST,
        name="wgrads",
    )(core, *lhs, *normed2, *upstream, *others)


def wgrad_out_body(count, core_ref, right_ref, *refs):
    keep_ref, send_ref = refs[count:]
    right = right_ref[...]
    first = core_ref[0] == 0
    at = 0
    for ref in refs[:count]:
        x = dg(ref[...], right, TN).astype(BF)
        rows, half = x.shape[0], x.shape[1] // 2
        keep_ref[at : at + rows, :] = jnp.where(first, x[:, :half], x[:, half:])
        send_ref[at : at + rows, :] = jnp.where(first, x[:, half:], x[:, :half])
        at += rows


def wgrad_out(lefts, right, core):
    rows, cols = sum(x.shape[1] for x in lefts), right.shape[1]
    vmem = pl.BlockSpec(memory_space=pltpu.VMEM)
    return pl.pallas_call(
        functools.partial(wgrad_out_body, len(lefts)),
        in_specs=[pl.BlockSpec(memory_space=pltpu.SMEM)] + [vmem] * (1 + len(lefts)),
        out_specs=[vmem] * 2,
        out_shape=[jax.ShapeDtypeStruct((rows, cols // 2), BF)] * 2,
        cost_estimate=COST,
        name="wgrad_out",
    )(core, right, *lefts)


def small_call(body, name, outs, scalar, *arrays):
    vmem = pl.BlockSpec(memory_space=pltpu.VMEM)
    return pl.pallas_call(
        body,
        in_specs=[pl.BlockSpec(memory_space=pltpu.SMEM)] + [vmem] * len(arrays),
        out_specs=[vmem] * len(outs),
        out_shape=[jax.ShapeDtypeStruct(s, t) for s, t in outs],
        cost_estimate=SMALL,
        name=name,
    )(scalar, *arrays)


def add(x, y):
    return (x.astype(F32) + y.astype(F32)).astype(BF)


class Sums:
    def __init__(self):
        self.count = lax.axis_size("dp")
        self.bits = self.count.bit_length() - 1
        self.index = lax.axis_index("dp").astype(jnp.int32)

    def bit(self, b):
        return (self.index >> b) & 1

    def swap(self, x, b):
        return lax.ppermute(x, "dp", [(i, i ^ (1 << b)) for i in range(self.count)])

    def halves(self, x, b, axis):
        half = x.shape[axis] // 2
        low = self.bit(b) * half
        keep = lax.dynamic_slice_in_dim(x, low, half, axis)
        return keep, lax.dynamic_slice_in_dim(x, half - low, half, axis)

    def join(self, mine, got, b, axis):
        low = self.bit(b) == 0
        parts = [jnp.where(low, mine, got), jnp.where(low, got, mine)]
        return jnp.concatenate(parts, axis=axis)


class Order:
    def __init__(self):
        self.last = ()

    def __call__(self, function, *args):
        args, _ = lax.optimization_barrier((args, self.last))
        out = function(*args)
        self.last = tuple(jax.tree.leaves(out))
        return out

    def here(self, x):
        return after(x, *self.last)


class Total:
    def __init__(self, sums, do, halves, bits, axes, finish, also=None):
        self.sums, self.do, self.bits, self.axes = sums, do, bits, axes
        self.finish, self.also = finish, also
        self.x, send = halves
        self.flight = sums.swap(send, 0)
        self.stage = 0

    def step(self):
        sums, (b0, b1, b2), (a0, a1) = self.sums, self.bits, self.axes
        stage = self.stage
        self.stage += 1
        if stage < 2:
            b, axis = ((b0, a0), (b1, a1))[stage]

            def scatter(x, got, *more):
                if more:
                    x = self.also(add(x, got), *more)
                    return sums.halves(x, b, axis)
                x, got = sums.halves(x, b, axis), sums.halves(got, b, axis)
                return add(x[0], got[0]), add(x[1], got[1])

            more = self.also.more() if self.also and stage == 0 else ()
            self.x, send = self.do(scatter, self.x, self.flight, *more)
            self.flight = sums.swap(send, b)
        elif stage < 4:
            self.x = self.do(add, self.x, self.flight)
            self.flight = sums.swap(self.x, b2 if stage == 2 else b1)
        elif stage == 4:
            self.x = self.do(lambda x, got: sums.join(x, got, b1, a1), self.x, self.flight)
            self.flight = sums.swap(self.x, b0)
            self.other = sums.swap(self.x, 0)
        elif stage == 5:
            self.y = self.do.here(self.flight)
            self.do.last = (*self.do.last, self.y)
            self.flight = sums.swap(self.y, 0)
        else:
            self.result = self.do(
                lambda got, other, x, y: self.finish(x, y, other, got),
                self.flight, self.other, self.x, self.y,
            )
            return []
        return [self]


class Beside:
    def __init__(self):
        self.array = None

    def more(self):
        return (self.array,)

    def __call__(self, x, y):
        return jnp.concatenate([x, y], axis=1)


def place_body(plane, count, s_ref, *refs):
    parts, out_ref, wide, sems = refs[:count], refs[-3], refs[-2], refs[-1]
    out = out_ref if plane is None else out_ref.at[plane]
    quarter = wide.shape[2]
    copies = []
    for k, part in enumerate(parts):
        wide[k] = part[...].astype(F32)
        at = ((k >> 1) ^ s_ref[0]) * 2 + ((k & 1) ^ s_ref[1])
        columns = pl.ds(pl.multiple_of(at * quarter, quarter), quarter)
        copies.append(pltpu.make_async_copy(wide.at[k], out.at[:, columns], sems.at[k]))
        copies[-1].start()
    for copy in copies:
        copy.wait()


def place(where, parts, planes=None, plane=None, before=None):
    rows, quarter = parts[0].shape
    shape = (rows, 4 * quarter) if planes is None else (planes, rows, 4 * quarter)
    extra = [] if before is None else [before]
    anywhere = pl.BlockSpec(memory_space=pl.ANY)
    return pl.pallas_call(
        functools.partial(place_body, plane, len(parts)),
        in_specs=[pl.BlockSpec(memory_space=pltpu.SMEM)]
        + [pl.BlockSpec(memory_space=pltpu.VMEM)] * 4
        + [anywhere] * len(extra),
        out_specs=anywhere,
        out_shape=jax.ShapeDtypeStruct(shape, F32),
        scratch_shapes=[pltpu.VMEM((4, rows, quarter), F32), pltpu.SemaphoreType.DMA((4,))],
        input_output_aliases={5: 0} if extra else {},
        cost_estimate=COST,
        name="place",
    )(where, *parts, *extra)


def project_body(x_ref, gain_ref, w_ref, *refs):
    normed_ref, packed_ref = refs[-2:]
    x = x_ref[...].astype(F32)
    normed = (x * scale_of(x) * gain_ref[...]).astype(BF)
    normed_ref[...] = normed
    packed_ref[...] = dg(normed, w_ref[...], NN).astype(BF)


def project(slot, slots, x, gain, w, buffers):
    rows, model = x.shape
    cols = w.shape[1]
    blk = min(256, rows)
    steps = rows // blk
    extra = [] if buffers is None else list(buffers)
    at = lambda c: pl.BlockSpec((blk, c), lambda i: (slot * steps + i, 0))
    full = lambda s: pl.BlockSpec(s, lambda i: (0, 0))
    return pl.pallas_call(
        project_body,
        grid=(steps,),
        in_specs=[pl.BlockSpec((blk, model), lambda i: (i, 0)), full((1, model)), full(w.shape)]
        + [pl.BlockSpec(memory_space=pl.ANY)] * len(extra),
        out_specs=[at(model), at(cols)],
        out_shape=[
            jax.ShapeDtypeStruct((slots * rows, model), BF),
            jax.ShapeDtypeStruct((slots * rows, cols), BF),
        ],
        input_output_aliases={3: 0, 4: 1} if extra else {},
        cost_estimate=COST,
        name="project",
    )(x, gain.reshape(1, model), w, *extra)


def assemble_body(s_ref, *refs):
    out_ref = refs[-1]
    rows = refs[0].shape[0]
    for k, ref in enumerate(refs[:-1]):
        at = ((s_ref[0] ^ (k & 1)) * 2 + (s_ref[1] ^ (k >> 1))) * rows
        out_ref[pl.ds(pl.multiple_of(at, rows), rows), :] = ref[...]


def assemble(where, *pieces):
    rows, cols = pieces[0].shape
    return small_call(assemble_body, "assemble", [((4 * rows, cols), BF)], where, *pieces)[0]


def mix_body(parts, steps, x_ref, *refs):
    resid = x_ref[...].astype(F32)
    for part, weight in zip(refs[:parts], refs[parts : 2 * parts]):
        resid = resid + dg(part[...], weight[...], NN)
    refs = refs[2 * parts :]
    if steps == 0:
        refs[0][...] = resid
        return
    gain_ref, resid_ref, normed_ref = refs[:3]
    resid_ref[...] = resid
    normed = (resid * scale_of(resid) * gain_ref[...]).astype(BF)
    normed_ref[...] = normed
    for k, ref in enumerate(refs[3:]):

        @pl.when(pl.program_id(0) == k)
        def _(ref=ref):
            ref[...] = normed


def part_of(w, k, n):
    return pl.BlockSpec((n, w.shape[1]), lambda i: (k, 0))


def mix(blk, x, parts, weights, gain=None):
    rows, model = x.shape
    at = lambda c: pl.BlockSpec((blk, c), lambda i: (i, 0))
    full = lambda s: pl.BlockSpec(s, lambda i: (0, 0))
    steps = rows // blk
    shape = lambda n, t: jax.ShapeDtypeStruct((n, model), t)
    norm = gain is not None
    out = pl.pallas_call(
        functools.partial(mix_body, len(parts), steps if norm else 0),
        grid=(steps,),
        in_specs=[at(model)]
        + [at(p.shape[1]) for p in parts]
        + [part_of(w, k, n) for w, k, n in weights]
        + ([full((1, model))] if norm else []),
        out_specs=[at(model)] + ([at(model)] + [full((blk, model))] * steps if norm else []),
        out_shape=[shape(rows, F32)] + ([shape(rows, BF)] + [shape(blk, BF)] * steps if norm else []),
        cost_estimate=COST,
        name="mix",
    )(x, *parts, *[w for w, _, _ in weights], *([gain.reshape(1, model)] if norm else []))
    return (out[0], out[1], out[2:]) if norm else out[0]


def turn_body(parts, steps, weights, dy_ref, resid_ref, gain_ref, first_ref, *refs):
    rest, w_refs = refs[:parts], refs[parts : parts + weights]
    grad_ref, mixer_ref, gain_grad_ref = refs[parts + weights : parts + weights + 3]
    g_refs = refs[parts + weights + 3 :]
    grad = first_ref[...]
    for at in range(0, parts, steps):
        x = rest[at][...]
        for k in range(1, steps):
            x = jnp.where(pl.program_id(0) == k, rest[at + k][...], x)
        grad = grad + x.astype(F32)
    back, gain_grad = rms_back(resid_ref[...], gain_ref[...], grad)
    resid_grad = dy_ref[...].astype(F32) + back
    grad_ref[...] = resid_grad
    mixer = resid_grad.astype(BF)
    mixer_ref[...] = mixer
    gain_grad = jnp.sum(gain_grad.reshape(-1, 8, gain_grad.shape[-1]), axis=0)

    @pl.when(pl.program_id(0) == 0)
    def _():
        gain_grad_ref[...] = gain_grad

    @pl.when(pl.program_id(0) > 0)
    def _():
        gain_grad_ref[...] += gain_grad

    for w_ref, g_ref in zip(w_refs, g_refs):
        g_ref[...] = dg(mixer, w_ref[...], NT).astype(BF)


def turn(dy, resid, gain, first, rest, weights):
    rows, model = dy.shape
    blk = rest[0][0].shape[0]
    steps = rows // blk
    at = lambda c: pl.BlockSpec((blk, c), lambda i: (i, 0))
    full = lambda s: pl.BlockSpec(s, lambda i: (0, 0))
    rest = [x for r in rest for x in r]
    return pl.pallas_call(
        functools.partial(turn_body, len(rest), steps, len(weights)),
        grid=(steps,),
        in_specs=[at(model), at(model), full((1, model)), at(model)]
        + [full((blk, model)) for _ in rest]
        + [part_of(w, k, n) for w, k, n in weights],
        out_specs=[at(model), at(model), full((8, model))] + [at(n) for _, _, n in weights],
        out_shape=[
            jax.ShapeDtypeStruct((rows, model), F32),
            jax.ShapeDtypeStruct((rows, model), BF),
            jax.ShapeDtypeStruct((8, model), F32),
        ]
        + [jax.ShapeDtypeStruct((rows, n), BF) for _, _, n in weights],
        cost_estimate=COST,
        name="turn",
    )(dy, resid, gain.reshape(1, model), first, *rest, *[w for w, _, _ in weights])


def scale_of(rows):
    return lax.rsqrt(jnp.mean(rows * rows, axis=-1, keepdims=True) + EPSILON)


def rms_back(rows, gain, grad):
    r = scale_of(rows)
    n = rows * r
    scaled = grad * gain
    back = r * (scaled - n * jnp.mean(scaled * n, axis=-1, keepdims=True))
    return back, grad * n


def order_matrix(heads, qw):
    width = 2 * F + V
    src = lax.broadcasted_iota(jnp.int32, (heads * width, 2 * qw + heads * V), 0)
    dst = lax.broadcasted_iota(jnp.int32, (heads * width, 2 * qw + heads * V), 1)
    head, part = src // width, src % width
    target = jnp.where(
        part < F,
        head * F + part,
        jnp.where(part < 2 * F, qw + head * F + part - F, 2 * qw + head * V + part - 2 * F),
    )
    return (target == dst).astype(BF)


def per_device(
    tokens, norm1_gain, w_qkv, w_out, norm2_gain, w_gate_up, w_down, cotangent, old_mean, momentum
):
    rows, model = tokens.shape
    group = lax.axis_size("tensor")
    length = rows * group
    heads = w_qkv.shape[1] // (2 * F + V)
    hidden_units = w_down.shape[0]
    qw = -(-heads * F // LANES) * LANES
    me = lax.axis_index("tensor")
    me_arr = me.astype(jnp.int32).reshape(1)
    blk = min(256, rows)
    per = rows // blk
    sums = Sums()

    def swap(x, r):
        return lax.ppermute(x, "tensor", [(i, i ^ r) for i in range(group)])

    fast = group == 2 and sums.bits == 4 and heads * V == model // 2 and hidden_units % 32 == 0
    core, y_bit, z_bit = sums.bit(0), sums.bit(1), sums.bit(2)
    core_arr = core.reshape(1)
    others = range(1, group)
    do = Order()
    step = max(rows // 2, 128)
    cuts = range(0, rows, step)

    arrived = [swap(tokens, r) for r in others]
    order = order_matrix(heads, qw)
    w_ordered = do(lambda w: dg(w, order, NN).astype(BF), w_qkv)
    quarter = w_out.shape[0] // 4
    buffers = do(lambda x, w: project(0, group, x, norm1_gain, w, None), tokens, w_ordered)
    upstream = {(0, 0): cotangent}

    def cut_inputs(dy, w, *_):
        low = (2 * y_bit + core) * quarter
        piece = lax.dynamic_slice_in_dim(w, low, quarter, 0) if fast else w
        return piece, [dy[low : low + step] for low in cuts]

    w_piece, dy_cuts = do(cut_inputs, cotangent, w_out, *arrived)
    if fast:
        piece = swap(w_piece, 1)
    else:
        w_rest = [swap(w_out, r) for r in others]
    for r in others:
        upstream[r, 0] = swap(dy_cuts[0], r)
    for r in others:
        buffers = do(
            lambda x, *b, r=r: project(r, group, x, norm1_gain, w_ordered, b), arrived[r - 1], *buffers
        )
    normed, packed = buffers

    pairs = heads // 2
    groups = 2 if pairs % 2 == 0 else 1
    each = pairs // groups
    span = each * LANES
    attended, crossed = [], []
    for k in range(groups):
        attended.append(
            do(lambda x, k=k: attend_fwd(x, me_arr, heads, qw, blk, per, k * each, each), packed)
        )
        for r in others:
            crossed.append((k, r, swap(attended[k][1][(r - 1) * rows : r * rows], r)))
        if fast and k == 0:
            piece = do.here(piece)
            piece_y = sums.swap(piece, 1)
            piece_core = sums.swap(piece, 0)
    att_own, att_sent, attf, den, den_sum = zip(*attended)
    upstream_first = do.here(tuple(upstream[r, 0] for r in others))
    do.last = (*do.last, *upstream_first)
    if fast:
        piece_y = do.here(piece_y)
        piece_both = sums.swap(piece_y, 0)
        place_of = jnp.stack([y_bit, core])
        w_rest, _ = do(
            lambda c, x, y, p, q: (assemble(place_of, p, q, x, y), c),
            [x for k, _, x in crossed if k == 0], piece_core, piece_both, piece, piece_y,
        )
        w_rest = [w_rest]

    parts = list(att_own) + [x for _, _, x in crossed]
    blocks_of = [(0, k) for k in range(groups)] + [(r, k) for k, r, _ in crossed]
    with_blocks = lambda ws, at: [(ws[r], k, span) for r, k in at]
    for low, dy_cut in zip(cuts[1:], dy_cuts[1:]):
        for r in others:
            upstream[r, low] = swap(do.here(after(dy_cut, *parts)), r)
    resid, own2, own2_cuts = do(
        lambda x, w: mix(step, tokens, x, with_blocks(w, blocks_of), norm2_gain),
        parts, [w_out, *w_rest],
    )

    w_gate_up = jnp.swapaxes(w_gate_up, 1, 2)
    blocks = [(0, 0)] + [(r, low) for r in others for low in cuts]
    normed2, waiting = [own2], own2
    buffers = ()
    out_parts, back_parts = [], []
    for at, (r, low) in enumerate(blocks):
        if r > 0:
            x = own2_cuts[low // step]
            normed2.append(swap(x if at == 1 else after(x, waiting), r))
        kind = F32 if r == 0 else BF
        taken = [dy for (q, _), dy in upstream.items() if q > 0] if at == 1 else []
        *buffers, out_part, back_part = do(
            lambda x, dy, b, t, r=r, low=low, kind=kind: ffn(
                r * rows + low, length, x, dy, 0, w_gate_up, w_down, b or None, kind
            ),
            normed2[-1],
            upstream[r, low],
            buffers,
            taken,
        )
        if at == 0:
            waiting, first_out, first_back = out_part, out_part, back_part
        else:
            out_parts.append((out_part, r))
            back_parts.append((r, low, swap(back_part, r)))
    hidden, gate_grad, up_grad = buffers
    dy_all = [upstream[k] for k in blocks]
    back_parts = [[x for q, _, x in back_parts if q == r] for r in others]

    def finish_output(resid, first_out, *got):
        output = resid + first_out
        got = got[::-1]
        for r in others:
            count = len(cuts)
            part = got[(r - 1) * count : r * count]
            output = output + jnp.concatenate(part, axis=0).astype(F32)
        return output.astype(BF)

    def finish_norm1(p, resid_grad, *got):
        grad = dg(p[:rows], w_ordered, NT)
        for x in got:
            grad = grad + x.astype(F32)
        back, gain_grad = rms_back(tokens.astype(F32), norm1_gain, grad)
        return resid_grad + back, jnp.sum(gain_grad, axis=0)

    def halve(x, got):
        half = x.shape[0] // 2
        return add(x[:half], got[:half]), add(x[half:], got[half:])

    def qkv_halves(normed, packed_grad):
        keep, send = sums.halves(normed, 0, 1)
        return dg(keep, packed_grad, TN).astype(BF), dg(send, packed_grad, TN).astype(BF)

    def both(x, y, x_other, y_other):
        mine, theirs = sums.join(x, y, 1, 0), sums.join(x_other, y_other, 1, 0)
        cols = packed.shape[1]
        qkv = sums.join(mine[:, :cols], theirs[:, :cols], 0, 0)
        out = sums.join(mine[:, cols:], theirs[:, cols:], 0, 1)
        return dg(qkv, order, NT), out.astype(F32)

    links = [lambda x, r=r: swap(x, 1 << r) for r in range(group.bit_length() - 1)]
    links += [lambda x, b=b: sums.swap(x, b) for b in range(sums.bits)]
    by_y, by_z = jnp.stack([core, y_bit]), jnp.stack([core, z_bit])
    beside = Beside()
    now = {"bwd": 0, "packed_grad": None, "w": 0, "link": 0}
    chains = {}

    def make_ffn():
        halves = do(
            lambda lhs, n, dy, m: wgrads(lhs, n, dy, core_arr, *m),
            (gate_grad, up_grad, hidden), normed2, dy_all, [x[0] for x in back_parts],
        )
        finish = lambda *x: place(by_y, x, 2, 0, now.get("pair"))
        chains["G"] = Total(sums, do, halves[:2], (1, 2, 3), (1, 1), finish)
        finish = lambda *x: place(by_y, x, 2, 1, now.get("pair"))
        chains["U"] = Total(sums, do, halves[2:4], (1, 2, 3), (1, 1), finish)
        finish = lambda *x: place(by_z, x)
        chains["D"] = Total(sums, do, halves[4:], (2, 3, 1), (1, 1), finish)

    def make_qkv():
        halves = do(qkv_halves, normed, now["packed_grad"])
        chains["Q"] = Total(sums, do, halves, (1, 2, 3), (0, 0), both, beside)

    def step_of(name):
        def step():
            chains[name].step()
            if name in "GU" and chains[name].stage == 7:
                now["pair"] = chains[name].result

        return step

    def turn_rows():
        turned = [(r, k) for r in range(group) for k in range(groups)]
        now["resid_grad"], now["mixer"], now["gain2"], *g_all = do(
            lambda *x: turn(*x[:2], norm2_gain, x[2], x[3], with_blocks(x[4], turned)),
            cotangent, resid, first_back, back_parts, [w_out, *w_rest],
        )
        now["g_own"], now["g_sent"] = g_all[:groups], []
        for k in range(groups):
            x = [swap(g_all[r * groups + k], r) for r in others]
            now["g_sent"].append(x[0] if group == 2 else jnp.concatenate(x, axis=0))

    def make_out():
        now["wx"], send = do(
            lambda m, p, *_: wgrad_out(p, m, core_arr), now["mixer"], parts, *reversed(now["g_sent"])
        )
        now["w_flight"] = sums.swap(send, 0)

    def step_out():
        now["w"] += 1
        if now["w"] == 1:
            now["wx"], send = do(halve, now["wx"], now["w_flight"])
            now["w_flight"] = swap(send, 1)
        else:
            beside.array = do(add, now["wx"], now["w_flight"])

    def backward():
        k = now["bwd"]
        now["bwd"] += 1
        before = [] if k == 0 else [now["packed_grad"]]
        now["packed_grad"] = do(
            lambda g, s, f, d, *b: attend_bwd(
                packed, g, s, f, d, me_arr, qw, rows, 1, k * each, each, *b
            ),
            now["g_own"][k], now["g_sent"][k], attf[k], den[k], *before,
        )

    def send_tokens():
        now["back1"] = []
        for r in others:
            part = do(
                lambda p, r=r: dg(p[r * rows : (r + 1) * rows], w_ordered, NT).astype(BF),
                now["packed_grad"],
            )
            now["back1"].append(swap(part, r))

    def finish_tokens():
        now["input_grad"], gain1_grad = do(
            finish_norm1, now["packed_grad"], now["resid_grad"], *now["back1"]
        )
        denom_local = sum(jnp.sum(d) for d in den_sum) * (0.5 / V)
        small = jnp.concatenate(
            [gain1_grad, jnp.sum(now["gain2"], axis=0), jnp.full((model,), denom_local / model)]
        )
        now["small"] = small.reshape(3 * model // LANES, LANES)
        now["flight"] = links[0](now["small"])

    def step_small():
        now["small"] = do(lambda x, y: x + y, now["small"], now["flight"])
        now["link"] += 1
        if now["link"] < len(links):
            now["flight"] = links[now["link"]](now["small"])

    def send_rows():
        now["got_out"] = [swap(do.here(x), k) for x, k in out_parts]

    def finish_rows():
        now["output"] = do(finish_output, resid, first_out, *reversed(now["got_out"]))

    steps = dict(
        g=make_ffn, q=make_qkv, t=turn_rows, w=make_out, W=step_out,
        A=backward, K=send_tokens, N=finish_tokens, s=step_small, O=send_rows, o=finish_rows,
        G=step_of("G"), U=step_of("U"), D=step_of("D"), Q=step_of("Q"),
    )
    for name in FAST if fast else "t" + "A" * groups + "KNOo" + "s" * len(links):
        steps[name]()
    input_grad, output, mixer_own = now["input_grad"], now["output"], now["mixer"]
    packed_grad = now["packed_grad"]
    small = now["small"].reshape(3, model)
    denom_total = jnp.sum(small[2])

    if fast:
        grad_gate_up, grad_down = now["pair"], chains["D"].result
        grad_qkv, grad_out = chains["Q"].result
    else:
        mixer_grad = jnp.concatenate([mixer_own] + [swap(mixer_own, r) for r in others], axis=0)
        att = jnp.concatenate(
            [jnp.concatenate(att_own, axis=1), jnp.concatenate(att_sent, axis=1)], axis=0
        )
        all_normed2 = jnp.concatenate(normed2, axis=0)
        all_upstream = jnp.concatenate(dy_all, axis=0)
        grad_down = dg(hidden, all_upstream, TN)
        grad_gate = dg(gate_grad, all_normed2, TN)
        grad_up = dg(up_grad, all_normed2, TN)
        grad_out = dg(att, mixer_grad, TN)
        grad_qkv = dg(dg(normed, packed_grad, TN).astype(BF), order, NT)
        grad_qkv, grad_out, grad_gate, grad_up, grad_down = lax.psum(
            (grad_qkv, grad_out, grad_gate, grad_up, grad_down), "dp"
        )
        grad_gate_up = jnp.stack([grad_gate, grad_up])
    grad_gate_up = jnp.swapaxes(grad_gate_up, 1, 2)

    rows_all = length * lax.axis_size("dp")
    per_row = heads * group * length
    mean_value = denom_total / rows_all / per_row
    new_mean = momentum * old_mean + (1.0 - momentum) * mean_value
    return (
        output,
        input_grad,
        small[0],
        grad_qkv,
        grad_out,
        small[1],
        grad_gate_up,
        grad_down,
        new_mean,
    )


def solution(mesh):
    rows = P(("dp", "tensor"), None)
    return jax.shard_map(
        per_device,
        mesh=mesh,
        in_specs=(
            rows, P(), P(None, "tensor"), P("tensor", None), P(),
            P(None, None, "tensor"), P("tensor", None), rows, P(), P(),
        ),
        out_specs=(
            rows, rows, P(), P(None, "tensor"), P("tensor", None), P(),
            P(None, None, "tensor"), P("tensor", None), P(),
        ),
        check_vma=False,
    )
```
